32 devices in a mesh: seq: 4 (over z), tp: 8 (over y, x, core).
Axes of the slice: x: 2, y: 2, z: 4, core: 2. Of those that a mesh axis runs over, the one named last changes fastest.
Arguments:
- tokens: bfloat16 [1024, 8192], P('tp', 'seq'), may hold values from -6 to 6
- gate_weight: bfloat16 [8192, 14336], P('seq', 'tp'), may hold values from -0.0625 to 0.0625
- up_weight: bfloat16 [8192, 14336], P('seq', 'tp'), may hold values from -0.0625 to 0.0625
- down_pool: bfloat16 [64, 64, 8192], P('tp', None, 'seq'), may hold values from -0.0625 to 0.0625
- up_pool: bfloat16 [64, 2, 64, 14336], P('seq', None, None, 'tp'), may hold values from -0.75 to 0.75
- req_len: int32 [4], replicated, may hold values from 1 to 4, 8 in all
- req_adapter: int32 [4], replicated, may hold values from 0 to 63
- owner_slot: int32 [64], replicated, may hold values from 0 to 63, each once
Outputs:
- hidden: bfloat16 [1024, 14336], P('seq', 'tp')
The draws below stay inside these ranges and needn't reach their ends.
Inputs may be any that keep to these rules, and one draw needn't show every extreme that they name: `req_len`: lengths of the requests in segments, summing to 8; the longest is exactly 4. `req_adapter`: adapter ids; an adapter may serve several requests. `owner_slot`: each pool slot once.
All inputs are finite; a program needn't handle non-finite values.
Results may differ from the reference program's by a relative error of at most 0.015.
Values may be sent and summed in bfloat16 or wider, within the bound.
No kernel may reach another device: no remote copies, remote signals or barrier semaphores. Data moves between devices by JAX's collectives and lax.ppermute only.
A program may use at most 128 MiB of HBM per device.

```python
import math
import jax
import jax.numpy as jnp
import numpy as np
from jax import lax

D = 8192
HIDDEN_SHARD = 14336
RANK = 64
SEG_ROWS = 128
SEGS = 8
TOKEN_ROWS_ALL = 1024
REQS = 4
ADAPTERS = 64
N_SEQ = 4


def with_ends(drawn, stream_key, smallest, largest):
    longest = drawn.shape.index(max(drawn.shape))
    spots = []
    for shift in (0, 1):
        where = [jax.random.randint(jax.random.fold_in(stream_key, axis), (), 0, length) for axis, length in enumerate(drawn.shape)]
        where[longest] = (where[longest] + shift) % drawn.shape[longest]
        spots.append(tuple(where))
    return drawn.at[spots[0]].set(smallest).at[spots[1]].set(largest)


def shard_levels(stream_key, extent, pieces, low, largest):
    level = 1.0
    for dim, blocks in pieces:
        heights = jax.random.uniform(jax.random.fold_in(jax.random.fold_in(stream_key, 6), dim), (blocks,), jnp.float32, low / len(pieces), largest / len(pieces))
        level = level * jnp.repeat(jnp.exp(heights), extent[dim] // blocks).reshape((-1,) + (1,) * (len(extent) - 1 - dim))
    return level


def rank_bounds(count, slope):
    portions = [(1 << 20) // math.isqrt(rank ** slope) + 1 for rank in range(1, count + 1)]
    scale = 1 + sum(portions) // (1 << 30)
    return np.cumsum(np.array([max(1, weight // scale) for weight in portions]))


def skewed_ids(own_key, shape, count, slope):
    listing = rank_bounds(count, slope)
    ticket = jax.random.randint(jax.random.fold_in(own_key, 1), shape, 0, int(listing[count - 1]))
    standing = jnp.searchsorted(jnp.asarray(listing, jnp.int32), ticket, side="right")
    return jax.random.permutation(jax.random.fold_in(own_key, 2), count)[standing].astype(jnp.int32)


def profile(amount, total, bound, lean):
    portions = [(1 << 20) // math.isqrt(rank ** lean) + 1 for rank in range(2, amount + 1)]
    surplus, given = total - bound - (amount - 1), [1] * (amount - 1)
    while surplus > 0:
        candidates = [i for i in range(amount - 1) if given[i] < bound]
        whole, remaining = sum([portions[i] for i in candidates]), surplus
        for i in candidates:
            more = min(bound - given[i], max(1, remaining * portions[i] // whole), surplus)
            given[i] = given[i] + more
            surplus = surplus - more
    return np.array([bound] + given)


def uneven_parts(key, count, total, bound, lean):
    if count == 2:
        one = jax.random.randint(key, (), max(1, total - bound), min(bound, total - 1) + 1)
        return jnp.stack([one, total - one])
    lengths = jnp.asarray(profile(count, total, bound, lean), jnp.int32)
    couples = (count - 1) // 2
    source_of, sink = lengths[1:1 + 2 * couples:2], lengths[2:2 + 2 * couples:2]
    margin = jnp.minimum(source_of - 1, bound - sink)
    moved = jax.random.randint(jax.random.fold_in(key, 1), (couples,), 0, 1 << 20) % (margin + 1)
    lengths = lengths.at[1:1 + 2 * couples:2].set(source_of - moved).at[2:2 + 2 * couples:2].set(sink + moved)
    return lengths[jax.random.permutation(jax.random.fold_in(key, 2), count)]


def noise(stream_key, extent, scale, limit, split=(), kind=jnp.bfloat16):
    drawn = jax.random.normal(stream_key, extent, jnp.float32) * scale
    if len(split) > 0:
        drawn = shard_levels(stream_key, extent, split, -0.22, 0.18) * drawn
    return jnp.clip(drawn, min=-limit, max=limit).astype(kind)


def setup_inputs(seed: int = 0) -> dict:
    key_list = jax.random.split(jax.random.key(seed), 9)
    tokens = noise(key_list[0], (TOKEN_ROWS_ALL, D), 1.0, 6.0, ((0, 8), (1, 4)))
    gate_weight = noise(key_list[1], (D, HIDDEN_SHARD), D ** -0.5, 0.0625, ((0, 4), (1, 8)))
    up_weight = noise(key_list[2], (D, HIDDEN_SHARD), D ** -0.5, 0.0625, ((0, 4), (1, 8)))
    down_pool = noise(key_list[3], (ADAPTERS, RANK, D), D ** -0.5, 0.0625, ((0, 8), (2, 4)))
    up_pool = noise(key_list[4], (ADAPTERS, 2, RANK, HIDDEN_SHARD), RANK ** -0.5, 0.75, ((0, 4), (3, 8)))
    req_len = uneven_parts(key_list[5], REQS, SEGS, 4, 1).astype(jnp.int32)
    req_adapter = with_ends(skewed_ids(key_list[6], (REQS,), ADAPTERS, 2), jax.random.fold_in(key_list[6], 3), 0, ADAPTERS - 1).astype(jnp.int32)
    owner_slot = jax.random.permutation(key_list[7], ADAPTERS).astype(jnp.int32)
    return dict(tokens=tokens, gate_weight=gate_weight, up_weight=up_weight, down_pool=down_pool, up_pool=up_pool, req_len=req_len, req_adapter=req_adapter, owner_slot=owner_slot)


low_rank_scale = 0.5


def reference(tokens, gate_weight, up_weight, down_pool, up_pool, req_len, req_adapter, owner_slot):
    ends = jnp.cumsum(req_len).astype(jnp.int32)
    segment = jnp.arange(SEGS, dtype=jnp.int32)
    seg_request = jnp.sum((ends[None, :] <= segment[:, None]).astype(jnp.int32), axis=1).astype(jnp.int32)
    seg_slot = owner_slot[req_adapter[seg_request]]
    width = D // N_SEQ
    gate_preactivation = jnp.zeros((TOKEN_ROWS_ALL, HIDDEN_SHARD), jnp.float32)
    up_preactivation = jnp.zeros((TOKEN_ROWS_ALL, HIDDEN_SHARD), jnp.float32)
    inner = jnp.zeros((SEGS, SEG_ROWS, RANK), jnp.float32)
    picked_down = down_pool[seg_slot]
    for block in range(N_SEQ):
        cols = tokens[:, block * width:(block + 1) * width]
        downs = picked_down[:, :, block * width:(block + 1) * width].astype(jnp.float32)
        segx = cols.reshape(SEGS, SEG_ROWS, width).astype(jnp.float32)
        inner_part = lax.optimization_barrier(jnp.einsum("kqd,krd->kqr", segx, downs).astype(jnp.bfloat16))
        inner = inner + inner_part.astype(jnp.float32)
        gate_part = jnp.dot(cols, gate_weight[block * width:(block + 1) * width], preferred_element_type=jnp.float32)
        up_part = jnp.dot(cols, up_weight[block * width:(block + 1) * width], preferred_element_type=jnp.float32)
        gate_part = lax.optimization_barrier(gate_part.astype(jnp.bfloat16))
        up_part = lax.optimization_barrier(up_part.astype(jnp.bfloat16))
        gate_preactivation = gate_preactivation + gate_part.astype(jnp.float32)
        up_preactivation = up_preactivation + up_part.astype(jnp.float32)
    inner_iteration = lax.optimization_barrier(inner.astype(jnp.bfloat16)).astype(jnp.float32)
    up_outputs = up_pool[seg_slot].astype(jnp.float32)
    low_rank_delta = jnp.einsum("vcz,vwzd->vcwd", inner_iteration, up_outputs).reshape(TOKEN_ROWS_ALL, 2, HIDDEN_SHARD)
    gate_preactivation = gate_preactivation + low_rank_scale * low_rank_delta[:, 0]
    up_preactivation = up_preactivation + low_rank_scale * low_rank_delta[:, 1]
    return (jax.nn.silu(gate_preactivation) * up_preactivation).astype(jnp.bfloat16)
```

```python
import jax
import jax.numpy as jnp
from jax import lax
from jax.sharding import PartitionSpec as P

SEG_ROWS = 128
SUB_BLOCKS = 2

low_rank_scale = 0.5


def segment_slots(req_len, req_adapter, owner_slot, segs):
    reqs = req_len.shape[0]
    order = jnp.arange(reqs, dtype=jnp.int32)
    ends = jnp.sum(jnp.where(order[:, None] <= order[None, :], req_len[:, None], 0), axis=0)
    segment = jnp.arange(segs, dtype=jnp.int32)
    seg_request = jnp.sum((ends[None, :] <= segment[:, None]).astype(jnp.int32), axis=1)
    adapter = jnp.sum(jnp.where(seg_request[:, None] == order[None, :], req_adapter[None, :], 0), axis=1)
    ids = jnp.arange(owner_slot.shape[0], dtype=jnp.int32)
    return jnp.sum(jnp.where(adapter[:, None] == ids[None, :], owner_slot[None, :], 0), axis=1)


def swap(x, axis, size, mask):
    return lax.ppermute(x, axis, [(i, i ^ mask) for i in range(size)])


def gather_rows(x, ntp):
    me = lax.axis_index("tp")
    mine = [x] + [swap(x, "tp", ntp, 2 * m) for m in range(1, ntp // 2)]
    out = jnp.zeros((ntp,) + x.shape, x.dtype)
    both = [(m, mine[m], swap(mine[m], "tp", ntp, 1)) for m in range(ntp // 2)]
    for m, own, other in both:
        out = lax.dynamic_update_slice_in_dim(out, own[None], me ^ (2 * m), 0)
        out = lax.dynamic_update_slice_in_dim(out, other[None], me ^ (2 * m) ^ 1, 0)
    return out


def sum_everywhere(x, nseq, ntp):
    x = x + swap(x, "tp", ntp, 1)
    x = sum([swap(x, "tp", ntp, 2 * m) for m in range(1, ntp // 2)], x)
    parts = [lax.ppermute(x, "seq", [(i, (i + k) % nseq) for i in range(nseq)]) for k in range(1, nseq)]
    total = x.astype(jnp.float32)
    for part in parts:
        total = total + part.astype(jnp.float32)
    return total.astype(jnp.bfloat16)


def slot_chunk(slot, nseq):
    me = lax.axis_index("seq")
    half = me < nseq // 2
    far = jnp.where(half, nseq - 1 - me, me)
    near = slot - far
    far_chunk = jnp.where(half, nseq - 1 - slot, slot)
    near_chunk = jnp.where(half, near, nseq - 1 - near)
    chunk = jnp.where(slot < far, far_chunk, near_chunk)
    return jnp.where(slot == nseq - 1, me, chunk)


def scatter_line(p, nseq):
    def own(slot):
        return lax.dynamic_index_in_dim(p, slot_chunk(slot, nseq), 0, keepdims=False)

    last = nseq - 2
    arrived = {}
    for step in range(nseq - 1):
        for level in range(step + 1):
            slot = step - level if level < nseq // 2 else step
            send = own(slot)
            if level > 0:
                send = (send.astype(jnp.float32) + arrived[level - 1, step - 1].astype(jnp.float32)).astype(p.dtype)
            pairs = [(level, level + 1), (nseq - 1 - level, nseq - 2 - level)]
            arrived[level, step] = lax.ppermute(send, "seq", pairs)
    total = own(nseq - 1).astype(jnp.float32)
    for level in range(nseq - 1):
        total = total + arrived[level, last].astype(jnp.float32)
    return total


def shards(tokens, gate_weight, up_weight, down_pool, up_pool, req_len, req_adapter, owner_slot):
    nseq = lax.axis_size("seq")
    ntp = lax.axis_size("tp")
    segs = ntp
    seg_slot = segment_slots(req_len, req_adapter, owner_slot, segs)
    per_tp, rank, width = down_pool.shape
    per_seq = up_pool.shape[0]
    columns = gate_weight.shape[1]
    rows = SEG_ROWS // SUB_BLOCKS
    down_local = seg_slot - lax.axis_index("tp") * per_tp
    pick_down = (down_local[None, :] == jnp.arange(per_tp, dtype=jnp.int32)[:, None]).astype(jnp.float32)
    up_local = seg_slot - lax.axis_index("seq") * per_seq
    held_up = (up_local >= 0) & (up_local < per_seq)
    ups = jnp.take(up_pool, jnp.clip(up_local, 0, per_seq - 1), axis=0)
    downs = down_pool.reshape(per_tp * rank, width)
    out = []
    for j in range(SUB_BLOCKS):
        block = tokens[j * rows:(j + 1) * rows]
        gathered = gather_rows(block, ntp)
        flat = gathered.reshape(segs * rows, width)
        every = lax.dot_general(downs, flat, (((1,), (1,)), ((), ())), preferred_element_type=jnp.float32)
        mine = jnp.sum(
            every.reshape(per_tp, rank, segs, rows) * pick_down[:, None, :, None], axis=0
        ).astype(jnp.bfloat16)
        inner = sum_everywhere(mine.reshape(rank, segs * rows), nseq, ntp).reshape(rank, segs, rows)
        inner = jnp.where(held_up[None, :, None], inner, jnp.zeros_like(inner))
        sums = []
        for which, weight in enumerate((gate_weight, up_weight)):
            part = jnp.dot(flat, weight, preferred_element_type=jnp.float32).reshape(segs, rows, columns)
            lora = jnp.einsum("zkq,kzd->kqd", inner, ups[:, which], preferred_element_type=jnp.float32)
            part = (part + low_rank_scale * lora).astype(jnp.bfloat16)
            sums.append(scatter_line(part.reshape(nseq, segs // nseq * rows, columns), nseq))
        gate, up = sums
        out.append((jax.nn.silu(gate) * up).astype(jnp.bfloat16).reshape(segs // nseq, rows, columns))
    return jnp.concatenate(out, axis=1).reshape(segs // nseq * SEG_ROWS, columns)


def solution(mesh):
    placed = (
        P("tp", "seq"),
        P("seq", "tp"),
        P("seq", "tp"),
        P("tp", None, "seq"),
        P("seq", None, None, "tp"),
        P(),
        P(),
        P(),
    )
    return jax.shard_map(
        shards, mesh=mesh, in_specs=placed, out_specs=P("seq", "tp"), check_vma=False
    )
```

```python
import functools

import jax
import jax.numpy as jnp
from jax import lax
from jax.experimental import pallas as pl
from jax.experimental.pallas import tpu as pltpu
from jax.sharding import PartitionSpec as P

SEG_ROWS = 128
SPLIT = (32, 96)

low_rank_scale = 0.5


def segment_slots(req_len, req_adapter, owner_slot, segs):
    reqs = req_len.shape[0]
    order = jnp.arange(reqs, dtype=jnp.int32)
    ends = jnp.sum(jnp.where(order[:, None] <= order[None, :], req_len[:, None], 0), axis=0)
    segment = jnp.arange(segs, dtype=jnp.int32)
    seg_request = jnp.sum((ends[None, :] <= segment[:, None]).astype(jnp.int32), axis=1)
    adapter = jnp.sum(jnp.where(seg_request[:, None] == order[None, :], req_adapter[None, :], 0), axis=1)
    ids = jnp.arange(owner_slot.shape[0], dtype=jnp.int32)
    return jnp.sum(jnp.where(adapter[:, None] == ids[None, :], owner_slot[None, :], 0), axis=1)


def held(seg_slot, first, count):
    local = seg_slot - first
    here = (local >= 0) & (local < count)
    return jnp.clip(local, 0, count - 1), here.astype(jnp.int32)


def swap(x, axis, size, mask):
    return lax.ppermute(x, axis, [(i, i ^ mask) for i in range(size)])


def gather_rows(x, ntp):
    chips = [x] + [swap(x, "tp", ntp, 2 * m) for m in range(1, ntp // 2)]
    pieces = []
    for piece in chips:
        pieces += [piece, swap(piece, "tp", ntp, 1)]
    return pieces


def sum_tp(x, ntp):
    x = x + swap(x, "tp", ntp, 1)
    return sum([swap(x, "tp", ntp, 2 * m) for m in range(1, ntp // 2)], x)


def sum_seq(x, nseq):
    parts = [lax.ppermute(x, "seq", [(i, (i + k) % nseq) for i in range(nseq)]) for k in range(1, nseq)]
    total = x.astype(jnp.float32)
    for part in parts:
        total = total + part.astype(jnp.float32)
    return total.astype(jnp.bfloat16)


def assemble_kernel(segs, tab_ref, *refs):
    pieces, (down_ref, x_ref, inner_ref) = refs[:segs], refs[segs:]
    me = tab_ref[2, 0]
    for n, piece in enumerate(pieces):
        x_ref[me ^ n] = piece[...]
    for pair in range(segs // 2):
        halves = []
        for k in (2 * pair, 2 * pair + 1):
            product = lax.dot_general(
                x_ref[k], down_ref[tab_ref[0, k]], (((1,), (1,)), ((), ())), preferred_element_type=jnp.float32
            )
            halves.append(product * tab_ref[1, k].astype(jnp.float32))
        inner_ref[pair] = jnp.concatenate(halves, axis=1).astype(jnp.bfloat16)


def assemble(pieces, down_pool, table):
    segs = len(pieces)
    rows, width = pieces[0].shape
    rank = down_pool.shape[1]
    vmem = pl.BlockSpec(memory_space=pltpu.VMEM)
    return pl.pallas_call(
        functools.partial(assemble_kernel, segs),
        out_shape=(
            jax.ShapeDtypeStruct((segs, rows, width), jnp.bfloat16),
            jax.ShapeDtypeStruct((segs // 2, rows, 2 * rank), jnp.bfloat16),
        ),
        in_specs=[pl.BlockSpec(memory_space=pltpu.SMEM)] + [vmem] * (segs + 1),
        out_specs=(vmem, vmem),
        compiler_params=pltpu.CompilerParams(vmem_limit_bytes=32 << 20),
        cost_estimate=pl.CostEstimate(
            flops=2 * segs * rows * width * rank, bytes_accessed=4 * segs * rows * width, transcendentals=0
        ),
    )(table, *pieces, down_pool)


def project_kernel(segs, nseq, tab_ref, x_ref, inner_ref, gate_ref, up_ref, *refs):
    ups, out_ref = refs[:segs], refs[segs]
    rows, width = x_ref.shape[1:]
    rank = inner_ref.shape[2] // 2
    each = segs // nseq
    x = x_ref[...].reshape(segs * rows, width)
    lows = []
    for k in range(segs):
        inner = inner_ref[k // 2][:, (k % 2) * rank:(k % 2 + 1) * rank]
        scale = low_rank_scale * tab_ref[1, k].astype(jnp.float32)
        lows.append((inner, scale))
    for which, weight in enumerate((gate_ref, up_ref)):
        part = jnp.dot(x, weight[...], preferred_element_type=jnp.float32)
        for k, (inner, scale) in enumerate(lows):
            low = jnp.dot(inner, ups[k][0, which], preferred_element_type=jnp.float32)
            term = part[k * rows:(k + 1) * rows] + scale * low
            out_ref[k // each, which, k % each] = term.astype(jnp.bfloat16)


def project(x, inner, gate_weight, up_weight, up_pool, table, nseq):
    segs, rows, width = x.shape
    columns = gate_weight.shape[1]
    rank = up_pool.shape[2]
    tile = 256 if columns % 256 == 0 else 128
    each = segs // nseq

    def up_spec(k):
        return pl.BlockSpec((1, 2, rank, tile), lambda n, tab: (tab[0, k], 0, 0, n))

    return pl.pallas_call(
        functools.partial(project_kernel, segs, nseq),
        out_shape=jax.ShapeDtypeStruct((nseq, 2, each, rows, columns), jnp.bfloat16),
        grid_spec=pltpu.PrefetchScalarGridSpec(
            num_scalar_prefetch=1,
            grid=(columns // tile,),
            in_specs=[
                pl.BlockSpec((segs, rows, width), lambda n, tab: (0, 0, 0)),
                pl.BlockSpec(inner.shape, lambda n, tab: (0, 0, 0)),
                pl.BlockSpec((width, tile), lambda n, tab: (0, n)),
                pl.BlockSpec((width, tile), lambda n, tab: (0, n)),
            ]
            + [up_spec(k) for k in range(segs)],
            out_specs=pl.BlockSpec((nseq, 2, each, rows, tile), lambda n, tab: (0, 0, 0, 0, n)),
        ),
        compiler_params=pltpu.CompilerParams(vmem_limit_bytes=40 << 20),
        cost_estimate=pl.CostEstimate(
            flops=4 * segs * rows * width * columns, bytes_accessed=4 * width * columns, transcendentals=0
        ),
    )(table, x, inner, gate_weight, up_weight, *([up_pool] * segs))


def after(x, gate):
    return lax.optimization_barrier((x, gate))[0]


def shards(tokens, gate_weight, up_weight, down_pool, up_pool, req_len, req_adapter, owner_slot):
    nseq = lax.axis_size("seq")
    ntp = lax.axis_size("tp")
    seg_slot = segment_slots(req_len, req_adapter, owner_slot, ntp)
    me = lax.axis_index("tp")
    down_slot, down_here = held(seg_slot, me * down_pool.shape[0], down_pool.shape[0])
    up_slot, up_here = held(seg_slot, lax.axis_index("seq") * up_pool.shape[0], up_pool.shape[0])
    down_table = jnp.stack([down_slot, down_here, jnp.full_like(down_slot, me)])
    up_table = jnp.stack([up_slot, up_here])
    columns = gate_weight.shape[1]
    out = []
    start = 0
    shared = sent = None
    for rows in SPLIT:
        block = tokens[start:start + rows]
        if shared is not None:
            block = after(block, shared)
        pieces = gather_rows(block, ntp)
        if sent is not None:
            pieces = list(after(tuple(pieces), sent))
        x, mine = assemble(pieces, down_pool, down_table)
        flat = mine.reshape(-1, mine.shape[2])
        shared = sum_tp(flat, ntp)
        inner = sum_seq(shared, nseq).reshape(mine.shape)
        sent = project(x, inner, gate_weight, up_weight, up_pool, up_table, nseq)
        total = lax.psum_scatter(sent, "seq", scatter_dimension=0, tiled=True)[0].astype(jnp.float32)
        out.append((jax.nn.silu(total[0]) * total[1]).astype(jnp.bfloat16))
        start += rows
    return jnp.concatenate(out, axis=1).reshape(-1, columns)


def solution(mesh):
    placed = (
        P("tp", "seq"),
        P("seq", "tp"),
        P("seq", "tp"),
        P("tp", None, "seq"),
        P("seq", None, None, "tp"),
        P(),
        P(),
        P(),
    )
    return jax.shard_map(
        shards, mesh=mesh, in_specs=placed, out_specs=P("seq", "tp"), check_vma=False
    )
```

```python
import functools

import jax
import jax.numpy as jnp
from jax import lax
from jax.experimental import pallas as pl
from jax.experimental.pallas import tpu as pltpu
from jax.sharding import PartitionSpec as P

SEG_ROWS = 128
GROUPS = ((32,), (48, 48))

low_rank_scale = 0.5


def slots_of(segment, req_len, req_adapter, owner_slot):
    order = jnp.arange(req_len.shape[0], dtype=jnp.int32)
    ends = jnp.sum(jnp.where(order[:, None] <= order[None, :], req_len[:, None], 0), axis=0)
    seg_request = jnp.sum((ends[None, :] <= segment[:, None]).astype(jnp.int32), axis=1)
    adapter = jnp.sum(jnp.where(seg_request[:, None] == order[None, :], req_adapter[None, :], 0), axis=1)
    ids = jnp.arange(owner_slot.shape[0], dtype=jnp.int32)
    return jnp.sum(jnp.where(adapter[:, None] == ids[None, :], owner_slot[None, :], 0), axis=1)


def chunk_of(slot, nseq):
    me = lax.axis_index("seq")
    half = me < nseq // 2
    far = jnp.where(half, nseq - 1 - me, me)
    near = slot - far
    far_chunk = jnp.where(half, nseq - 1 - slot, slot)
    near_chunk = jnp.where(half, near, nseq - 1 - near)
    chunk = jnp.where(slot < far, far_chunk, near_chunk)
    return jnp.where(slot == nseq - 1, me, chunk)


def held(seg_slot, first, count):
    local = seg_slot - first
    here = (local >= 0) & (local < count)
    return jnp.clip(local, 0, count - 1), here.astype(jnp.int32)


def swap(x, axis, size, mask):
    return lax.ppermute(x, axis, [(i, i ^ mask) for i in range(size)])


def gather_rows(x, ntp):
    chips = [x] + [swap(x, "tp", ntp, 2 * m) for m in range(1, ntp // 2)]
    pieces = []
    for piece in chips:
        pieces += [piece, swap(piece, "tp", ntp, 1)]
    return pieces


def sum_tp(x, ntp):
    x = x + swap(x, "tp", ntp, 1)
    return sum([swap(x, "tp", ntp, 2 * m) for m in range(1, ntp // 2)], x)


def sum_seq(x, nseq):
    parts = [lax.ppermute(x, "seq", [(i, (i + k) % nseq) for i in range(nseq)]) for k in range(1, nseq)]
    total = x.astype(jnp.float32)
    for part in parts:
        total = total + part.astype(jnp.float32)
    return total.astype(jnp.bfloat16)


def assemble_kernel(segs, tab_ref, *refs):
    pieces, (down_ref, x_ref, inner_ref) = refs[:segs], refs[segs:]
    me = tab_ref[2, 0]
    for n, piece in enumerate(pieces):
        x_ref[tab_ref[3, me ^ n]] = piece[...]
    for pair in range(segs // 2):
        halves = []
        for k in (2 * pair, 2 * pair + 1):
            product = lax.dot_general(
                x_ref[tab_ref[3, k]], down_ref[tab_ref[0, k]], (((1,), (1,)), ((), ())), preferred_element_type=jnp.float32
            )
            halves.append(product * tab_ref[1, k].astype(jnp.float32))
        inner_ref[pair] = jnp.concatenate(halves, axis=1).astype(jnp.bfloat16)


def assemble(pieces, down_pool, table):
    segs = len(pieces)
    rows, width = pieces[0].shape
    rank = down_pool.shape[1]
    vmem = pl.BlockSpec(memory_space=pltpu.VMEM)
    return pl.pallas_call(
        functools.partial(assemble_kernel, segs),
        out_shape=(
            jax.ShapeDtypeStruct((segs, rows, width), jnp.bfloat16),
            jax.ShapeDtypeStruct((segs // 2, rows, 2 * rank), jnp.bfloat16),
        ),
        in_specs=[pl.BlockSpec(memory_space=pltpu.SMEM)] + [vmem] * (segs + 1),
        out_specs=(vmem, vmem),
        compiler_params=pltpu.CompilerParams(vmem_limit_bytes=32 << 20),
        cost_estimate=pl.CostEstimate(
            flops=2 * segs * rows * width * rank, bytes_accessed=4 * segs * rows * width, transcendentals=0
        ),
    )(table, *pieces, down_pool)


def project_kernel(segs, nseq, tab_ref, x_ref, inner_ref, gate_ref, up_ref, *refs):
    ups, outs, low_ref = refs[:segs], refs[segs:segs + nseq], refs[segs + nseq]
    rows, width = x_ref.shape[1:]
    lanes = inner_ref.shape[2]
    rank = lanes // 2
    each = segs // nseq

    @pl.when(pl.program_id(0) == 0)
    def _():
        low_ref[...] = jnp.zeros_like(low_ref)
        lane = lax.broadcasted_iota(jnp.int32, (rows, lanes), 1)
        for k in range(segs):
            seg = tab_ref[2, k]
            mine = (lane // rank == seg % 2) & (tab_ref[1, k] == 1)
            inner = jnp.where(mine, inner_ref[seg // 2].astype(jnp.float32), 0.0) * low_rank_scale
            turned = jnp.where(seg % 2 == k % 2, inner, pltpu.roll(inner, rank, 1))
            low_ref[pl.ds(k * rows, rows), pl.ds(k // 2 * lanes, lanes)] = turned.astype(jnp.bfloat16)

    x = x_ref[...].reshape(segs * rows, width)
    for which, weight in enumerate((gate_ref, up_ref)):
        part = jnp.dot(x, weight[...], preferred_element_type=jnp.float32)
        stacked = jnp.concatenate([up[0, which] for up in ups], axis=0)
        part = part + jnp.dot(low_ref[...], stacked, preferred_element_type=jnp.float32)
        part = part.astype(jnp.bfloat16)
        for k in range(segs):
            outs[k // each][which, k % each] = part[k * rows:(k + 1) * rows]


def project(x, inner, index, rows, gate_weight, up_weight, up_pool, table, nseq):
    segs, _, width = x.shape
    columns = gate_weight.shape[1]
    rank = up_pool.shape[2]
    tile = 256 if columns % 256 == 0 else 128
    each = segs // nseq

    def up_spec(k):
        return pl.BlockSpec((1, 2, rank, tile), lambda n, tab: (tab[0, k], 0, 0, n))

    return pl.pallas_call(
        functools.partial(project_kernel, segs, nseq),
        out_shape=[jax.ShapeDtypeStruct((2, each, rows, columns), jnp.bfloat16)] * nseq,
        grid_spec=pltpu.PrefetchScalarGridSpec(
            num_scalar_prefetch=1,
            grid=(columns // tile,),
            in_specs=[
                pl.BlockSpec((segs, rows, width), lambda n, tab: (0, index, 0)),
                pl.BlockSpec((inner.shape[0], rows, inner.shape[2]), lambda n, tab: (0, index, 0)),
                pl.BlockSpec((width, tile), lambda n, tab: (0, n)),
                pl.BlockSpec((width, tile), lambda n, tab: (0, n)),
            ]
            + [up_spec(k) for k in range(segs)],
            out_specs=[pl.BlockSpec((2, each, rows, tile), lambda n, tab: (0, 0, 0, n))] * nseq,
            scratch_shapes=[pltpu.VMEM((segs * rows, segs * rank), jnp.bfloat16)],
        ),
        compiler_params=pltpu.CompilerParams(vmem_limit_bytes=40 << 20),
        cost_estimate=pl.CostEstimate(
            flops=4 * segs * rows * width * columns, bytes_accessed=4 * width * columns, transcendentals=0
        ),
    )(table, x, inner, gate_weight, up_weight, *([up_pool] * segs))


def add(x, y):
    return (x.astype(jnp.float32) + y.astype(jnp.float32)).astype(x.dtype)


def scatter_line(own, nseq):
    last = nseq - 2
    arrived = {}
    for step in range(nseq - 1):
        for level in range(step + 1):
            slot = step - level if level < nseq // 2 else step
            send = own[slot]
            if level > 0:
                send = add(send, arrived[level - 1, step - 1])
            pairs = [(level, level + 1), (nseq - 1 - level, nseq - 2 - level)]
            arrived[level, step] = lax.ppermute(send, "seq", pairs)
    total = own[nseq - 1].astype(jnp.float32)
    for level in range(nseq - 1):
        total = total + arrived[level, last].astype(jnp.float32)
    return total


def after(x, gate):
    return lax.optimization_barrier((x, gate))[0]


def shards(tokens, gate_weight, up_weight, down_pool, up_pool, req_len, req_adapter, owner_slot):
    nseq = lax.axis_size("seq")
    ntp = lax.axis_size("tp")
    each = ntp // nseq
    me = lax.axis_index("tp")
    place = jnp.arange(ntp, dtype=jnp.int32)
    ordered = chunk_of(place // each, nseq) * each + place % each
    position = jnp.sum(jnp.where(ordered[:, None] == place[None, :], place[:, None], 0), axis=0)
    down_slot, down_here = held(
        slots_of(place, req_len, req_adapter, owner_slot), me * down_pool.shape[0], down_pool.shape[0]
    )
    up_slot, up_here = held(
        slots_of(ordered, req_len, req_adapter, owner_slot),
        lax.axis_index("seq") * up_pool.shape[0],
        up_pool.shape[0],
    )
    down_table = jnp.stack([down_slot, down_here, jnp.full_like(down_slot, me), position])
    up_table = jnp.stack([up_slot, up_here, ordered])
    columns = gate_weight.shape[1]
    out = []
    start = 0
    shared = sent = None
    for group in GROUPS:
        block = tokens[start:start + sum(group)]
        if shared is not None:
            block = after(block, shared)
        pieces = gather_rows(block, ntp)
        if sent is not None:
            pieces = list(after(tuple(pieces), sent[0]))
        x, mine = assemble(pieces, down_pool, down_table)
        flat = mine.reshape(-1, mine.shape[2])
        shared = sum_tp(flat, ntp)
        inner = sum_seq(shared, nseq).reshape(mine.shape)
        for index, rows in enumerate(group):
            sent = project(x, inner, index, rows, gate_weight, up_weight, up_pool, up_table, nseq)
            total = scatter_line(sent, nseq)
            out.append((jax.nn.silu(total[0]) * total[1]).astype(jnp.bfloat16))
        start += sum(group)
    return jnp.concatenate(out, axis=1).reshape(-1, columns)


def solution(mesh):
    placed = (
        P("tp", "seq"),
        P("seq", "tp"),
        P("seq", "tp"),
        P("tp", None, "seq"),
        P("seq", None, None, "tp"),
        P(),
        P(),
        P(),
    )
    return jax.shard_map(
        shards, mesh=mesh, in_specs=placed, out_specs=P("seq", "tp"), check_vma=False
    )
```

```python
import functools

import jax
import jax.numpy as jnp
from jax import lax
from jax.experimental import pallas as pl
from jax.experimental.pallas import tpu as pltpu
from jax.sharding import PartitionSpec as P

SEG_ROWS = 128
GROUPS = ((48,), (48, 32))
IN_FLIGHT = 2

low_rank_scale = 0.5


def slots_of(segment, req_len, req_adapter, owner_slot):
    order = jnp.arange(req_len.shape[0], dtype=jnp.int32)
    ends = jnp.sum(jnp.where(order[:, None] <= order[None, :], req_len[:, None], 0), axis=0)
    seg_request = jnp.sum((ends[None, :] <= segment[:, None]).astype(jnp.int32), axis=1)
    adapter = jnp.sum(jnp.where(seg_request[:, None] == order[None, :], req_adapter[None, :], 0), axis=1)
    ids = jnp.arange(owner_slot.shape[0], dtype=jnp.int32)
    return jnp.sum(jnp.where(adapter[:, None] == ids[None, :], owner_slot[None, :], 0), axis=1)


def chunk_of(slot, nseq):
    me = lax.axis_index("seq")
    half = me < nseq // 2
    far = jnp.where(half, nseq - 1 - me, me)
    near = slot - far
    far_chunk = jnp.where(half, nseq - 1 - slot, slot)
    near_chunk = jnp.where(half, near, nseq - 1 - near)
    chunk = jnp.where(slot < far, far_chunk, near_chunk)
    return jnp.where(slot == nseq - 1, me, chunk)


def held(seg_slot, first, count):
    local = seg_slot - first
    here = (local >= 0) & (local < count)
    return jnp.clip(local, 0, count - 1), here.astype(jnp.int32)


def swap(x, axis, size, mask):
    return lax.ppermute(x, axis, [(i, i ^ mask) for i in range(size)])


def gather_rows(x, ntp):
    chips = [x] + [swap(x, "tp", ntp, 2 * m) for m in range(1, ntp // 2)]
    pieces = []
    for piece in chips:
        pieces += [piece, swap(piece, "tp", ntp, 1)]
    return pieces


def sum_across(x, axis, size):
    steps = []
    mask = 1
    while mask < size:
        x = add(x, swap(x, axis, size, mask))
        steps.append(x)
        mask *= 2
    return steps


def assemble_kernel(segs, group, tab_ref, *refs):
    pieces, down_ref, xs, inner_ref = refs[:segs], refs[segs], refs[segs + 1:-1], refs[-1]
    me = tab_ref[2, 0]
    for n, piece in enumerate(pieces):
        start = 0
        for x_ref, rows in zip(xs, group):
            x_ref[tab_ref[3, me ^ n]] = piece[start:start + rows]
            start += rows
    start = 0
    for x_ref, rows in zip(xs, group):
        for pair in range(segs // 2):
            halves = []
            for k in (2 * pair, 2 * pair + 1):
                product = lax.dot_general(
                    x_ref[tab_ref[3, k]],
                    down_ref[tab_ref[0, k]],
                    (((1,), (1,)), ((), ())),
                    preferred_element_type=jnp.float32,
                )
                halves.append(product * tab_ref[1, k].astype(jnp.float32))
            inner_ref[pair, start:start + rows] = jnp.concatenate(halves, axis=1).astype(jnp.bfloat16)
        start += rows


def assemble(pieces, group, down_pool, table):
    segs = len(pieces)
    total, width = pieces[0].shape
    rank = down_pool.shape[1]
    vmem = pl.BlockSpec(memory_space=pltpu.VMEM)
    *xs, mine = pl.pallas_call(
        functools.partial(assemble_kernel, segs, group),
        out_shape=[jax.ShapeDtypeStruct((segs, rows, width), jnp.bfloat16) for rows in group]
        + [jax.ShapeDtypeStruct((segs // 2, total, 2 * rank), jnp.bfloat16)],
        in_specs=[pl.BlockSpec(memory_space=pltpu.SMEM)] + [vmem] * (segs + 1),
        out_specs=[vmem] * (len(group) + 1),
        compiler_params=pltpu.CompilerParams(vmem_limit_bytes=32 << 20),
        cost_estimate=pl.CostEstimate(
            flops=2 * segs * total * width * rank, bytes_accessed=4 * segs * total * width, transcendentals=0
        ),
    )(table, *pieces, down_pool)
    return xs, mine


def low_rank_kernel(slot, each, start, tab_ref, inner_ref, gate_ref, up_ref, *refs):
    ups, out_ref, low_ref = refs[:each], refs[each], refs[each + 1]
    lanes = inner_ref.shape[2]
    rank = lanes // 2
    rows = out_ref.shape[2]

    @pl.when(pl.program_id(0) == 0)
    def _():
        lane = lax.broadcasted_iota(jnp.int32, (rows, lanes), 1)
        for e in range(each):
            seg = tab_ref[2, slot * each + e]
            mine = (lane // rank == seg % 2) & (tab_ref[1, slot * each + e] == 1)
            inner = inner_ref[seg // 2][start:start + rows].astype(jnp.float32)
            low_ref[e] = (jnp.where(mine, inner, 0.0) * low_rank_scale).astype(jnp.bfloat16)

    for which, part_ref in enumerate((gate_ref, up_ref)):
        for e in range(each):
            factor = ups[e][0, which]
            low = jnp.dot(low_ref[e], jnp.concatenate([factor, factor], axis=0), preferred_element_type=jnp.float32)
            term = part_ref[e * rows:(e + 1) * rows].astype(jnp.float32) + low
            out_ref[which, e] = term.astype(jnp.bfloat16)


def add_low_rank(gate, up, inner, start, rows, slot, up_pool, table, each):
    columns = gate.shape[1]
    rank = up_pool.shape[2]
    tile = next(t for t in (896, 512, 256, 128) if columns % t == 0)

    def up_spec(e):
        return pl.BlockSpec((1, 2, rank, tile), lambda n, tab: (tab[0, slot * each + e], 0, 0, n))

    return pl.pallas_call(
        functools.partial(low_rank_kernel, slot, each, start),
        out_shape=jax.ShapeDtypeStruct((2, each, rows, columns), jnp.bfloat16),
        grid_spec=pltpu.PrefetchScalarGridSpec(
            num_scalar_prefetch=1,
            grid=(columns // tile,),
            in_specs=[
                pl.BlockSpec(inner.shape, lambda n, tab: (0, 0, 0)),
                pl.BlockSpec((each * rows, tile), lambda n, tab: (slot, n)),
                pl.BlockSpec((each * rows, tile), lambda n, tab: (slot, n)),
            ]
            + [up_spec(e) for e in range(each)],
            out_specs=pl.BlockSpec((2, each, rows, tile), lambda n, tab: (0, 0, 0, n)),
            scratch_shapes=[pltpu.VMEM((each, rows, 2 * rank), jnp.bfloat16)],
        ),
        compiler_params=pltpu.CompilerParams(vmem_limit_bytes=16 << 20),
        cost_estimate=pl.CostEstimate(
            flops=8 * each * rows * 2 * rank * columns,
            bytes_accessed=4 * each * (2 * rows + rank) * columns,
            transcendentals=0,
        ),
    )(table, inner, gate, up, *([up_pool] * each))


def add(x, y):
    return (x.astype(jnp.float32) + y.astype(jnp.float32)).astype(x.dtype)


def scatter_line(own, nseq, first_hops):
    last = nseq - 2
    arrived = {}
    for step in range(nseq - 1):
        for level in range(step + 1):
            slot = step - level if level < nseq // 2 else step
            send = own[slot]
            if level > 0:
                send = add(send, arrived[level - 1, step - 1])
            elif len(first_hops) >= IN_FLIGHT:
                send = after(send, first_hops[-IN_FLIGHT])
            pairs = [(level, level + 1), (nseq - 1 - level, nseq - 2 - level)]
            arrived[level, step] = lax.ppermute(send, "seq", pairs)
            if level == 0:
                first_hops.append(arrived[level, step])
    total = own[nseq - 1].astype(jnp.float32)
    for level in range(nseq - 1):
        total = total + arrived[level, last].astype(jnp.float32)
    return total


def after(x, gate):
    return lax.optimization_barrier((x, gate))[0]


def shards(tokens, gate_weight, up_weight, down_pool, up_pool, req_len, req_adapter, owner_slot):
    nseq = lax.axis_size("seq")
    ntp = lax.axis_size("tp")
    each = ntp // nseq
    me = lax.axis_index("tp")
    place = jnp.arange(ntp, dtype=jnp.int32)
    ordered = chunk_of(place // each, nseq) * each + place % each
    position = jnp.sum(jnp.where(ordered[:, None] == place[None, :], place[:, None], 0), axis=0)
    down_slot, down_here = held(
        slots_of(place, req_len, req_adapter, owner_slot), me * down_pool.shape[0], down_pool.shape[0]
    )
    up_slot, up_here = held(
        slots_of(ordered, req_len, req_adapter, owner_slot),
        lax.axis_index("seq") * up_pool.shape[0],
        up_pool.shape[0],
    )
    down_table = jnp.stack([down_slot, down_here, jnp.full_like(down_slot, me), position])
    up_table = jnp.stack([up_slot, up_here, ordered])
    columns = gate_weight.shape[1]
    out = []
    start = 0
    shared = sent = None
    first_hops = []
    for group in GROUPS:
        block = tokens[start:start + sum(group)]
        if shared is not None:
            block = after(block, shared)
        pieces = gather_rows(block, ntp)
        if sent is not None:
            pieces = list(after(tuple(pieces), sent[-1]))
        xs, mine = assemble(pieces, group, down_pool, down_table)
        steps = sum_across(mine.reshape(-1, mine.shape[2]), "tp", ntp)
        shared = steps[-1]
        inner = sum_across(shared, "seq", nseq)[-1].reshape(mine.shape)
        offset = 0
        ready = steps[0]
        for x, rows in zip(xs, group):
            x = after(x.reshape(-1, x.shape[2]), ready)
            gate, up = [
                jnp.dot(x, weight, preferred_element_type=jnp.float32).astype(jnp.bfloat16)
                for weight in (gate_weight, up_weight)
            ]
            sent = []
            for slot in range(nseq):
                given = after(inner, sent[-1]) if sent else inner
                sent.append(add_low_rank(gate, up, given, offset, rows, slot, up_pool, up_table, each))
            ready = sent[-1]
            total = scatter_line(sent, nseq, first_hops)
            out.append((jax.nn.silu(total[0]) * total[1]).astype(jnp.bfloat16))
            offset += rows
        start += sum(group)
    return jnp.concatenate(out, axis=1).reshape(-1, columns)


def solution(mesh):
    placed = (
        P("tp", "seq"),
        P("seq", "tp"),
        P("seq", "tp"),
        P("tp", None, "seq"),
        P("seq", None, None, "tp"),
        P(),
        P(),
        P(),
    )
    return jax.shard_map(
        shards, mesh=mesh, in_specs=placed, out_specs=P("seq", "tp"), check_vma=False
    )
```

```python
import functools

import jax
import jax.numpy as jnp
from jax import lax
from jax.experimental import pallas as pl
from jax.experimental.pallas import tpu as pltpu
from jax.sharding import PartitionSpec as P

SEG_ROWS = 128
GROUPS = ((48,), (80,))
AHEAD = 1 << 36

low_rank_scale = 0.5


def slots_of(segment, req_len, req_adapter, owner_slot):
    order = jnp.arange(req_len.shape[0], dtype=jnp.int32)
    ends = jnp.sum(jnp.where(order[:, None] <= order[None, :], req_len[:, None], 0), axis=0)
    seg_request = jnp.sum((ends[None, :] <= segment[:, None]).astype(jnp.int32), axis=1)
    adapter = jnp.sum(jnp.where(seg_request[:, None] == order[None, :], req_adapter[None, :], 0), axis=1)
    ids = jnp.arange(owner_slot.shape[0], dtype=jnp.int32)
    return jnp.sum(jnp.where(adapter[:, None] == ids[None, :], owner_slot[None, :], 0), axis=1)


def chunk_of(slot, nseq):
    me = lax.axis_index("seq")
    half = me < nseq // 2
    far = jnp.where(half, nseq - 1 - me, me)
    near = slot - far
    far_chunk = jnp.where(half, nseq - 1 - slot, slot)
    near_chunk = jnp.where(half, near, nseq - 1 - near)
    chunk = jnp.where(slot < far, far_chunk, near_chunk)
    return jnp.where(slot == nseq - 1, me, chunk)


def held(seg_slot, first, count):
    local = seg_slot - first
    here = (local >= 0) & (local < count)
    return jnp.clip(local, 0, count - 1), here.astype(jnp.int32)


def swap(x, axis, size, mask):
    return lax.ppermute(x, axis, [(i, i ^ mask) for i in range(size)])


def gather_rows(x, ntp):
    chips = [x] + [swap(x, "tp", ntp, 2 * m) for m in range(1, ntp // 2)]
    pieces = []
    for piece in chips:
        pieces += [piece, swap(piece, "tp", ntp, 1)]
    return pieces


def sum_one_step(x, axis, size):
    parts = [lax.ppermute(x, axis, [(i, (i + k) % size) for i in range(size)]) for k in range(1, size)]
    total = x.astype(jnp.float32)
    for part in parts:
        total = total + part.astype(jnp.float32)
    return total.astype(x.dtype)


def sum_beside(x, axis, size, beside):
    done = []
    mask = 1
    while mask < size:
        other = swap(x, axis, size, mask)
        if mask > 1 or axis != "tp":
            done.append(beside(x))
            other = after(other, done[-1]) if done[-1] is not None else other
        x = add(x, other)
        mask *= 2
    return x, done


def assemble_kernel(segs, group, tab_ref, *refs):
    pieces, down_ref, xs, inner_ref = refs[:segs], refs[segs], refs[segs + 1:-1], refs[-1]
    me = tab_ref[2, 0]
    for n, piece in enumerate(pieces):
        start = 0
        for x_ref, rows in zip(xs, group):
            x_ref[tab_ref[3, me ^ n]] = piece[start:start + rows]
            start += rows
    start = 0
    for x_ref, rows in zip(xs, group):
        for pair in range(segs // 2):
            halves = []
            for k in (2 * pair, 2 * pair + 1):
                product = lax.dot_general(
                    x_ref[tab_ref[3, k]],
                    down_ref[tab_ref[0, k]],
                    (((1,), (1,)), ((), ())),
                    preferred_element_type=jnp.float32,
                )
                halves.append(product * tab_ref[1, k].astype(jnp.float32))
            inner_ref[pair, start:start + rows] = jnp.concatenate(halves, axis=1).astype(jnp.bfloat16)
        start += rows


def assemble(pieces, group, down_pool, table, hint):
    segs = len(pieces)
    total, width = pieces[0].shape
    rank = down_pool.shape[1]
    vmem = pl.BlockSpec(memory_space=pltpu.VMEM)
    *xs, mine = pl.pallas_call(
        functools.partial(assemble_kernel, segs, group),
        out_shape=[jax.ShapeDtypeStruct((segs, rows, width), jnp.bfloat16) for rows in group]
        + [jax.ShapeDtypeStruct((segs // 2, total, 2 * rank), jnp.bfloat16)],
        in_specs=[pl.BlockSpec(memory_space=pltpu.SMEM)] + [vmem] * (segs + 1),
        out_specs=[vmem] * (len(group) + 1),
        compiler_params=pltpu.CompilerParams(vmem_limit_bytes=32 << 20),
        cost_estimate=pl.CostEstimate(flops=hint, bytes_accessed=4 * segs * total * width, transcendentals=0),
    )(table, *pieces, down_pool)
    return xs, mine


def project_kernel(x_ref, weight_ref, out_ref):
    out_ref[...] = jnp.dot(x_ref[...], weight_ref[...], preferred_element_type=jnp.float32).astype(jnp.bfloat16)


def project(x, weight, first, count, tile, hint=0):
    width = weight.shape[0]
    rows = x.shape[0]
    return pl.pallas_call(
        project_kernel,
        out_shape=jax.ShapeDtypeStruct((rows, count * tile), jnp.bfloat16),
        grid=(count,),
        in_specs=[
            pl.BlockSpec((rows, width), lambda n: (0, 0)),
            pl.BlockSpec((width, tile), lambda n: (0, first + n)),
        ],
        out_specs=pl.BlockSpec((rows, tile), lambda n: (0, n)),
        compiler_params=pltpu.CompilerParams(vmem_limit_bytes=16 << 20),
        cost_estimate=pl.CostEstimate(
            flops=hint or 2 * rows * width * count * tile, bytes_accessed=2 * width * count * tile, transcendentals=0
        ),
    )(x, weight)


def low_rank_kernel(first, each, start, widths, tab_ref, inner_ref, *refs):
    parts, ups, out_ref = refs[:2 * len(widths)], refs[2 * len(widths):-1], refs[-1]
    slot = first + pl.program_id(0)
    lanes = inner_ref.shape[2]
    rank = lanes // 2
    rows = out_ref.shape[3]
    lane = lax.broadcasted_iota(jnp.int32, (rows, lanes), 1)
    for e in range(each):
        seg = tab_ref[2, slot * each + e]
        mine = (lane // rank == seg % 2) & (tab_ref[1, slot * each + e] == 1)
        inner = inner_ref[seg // 2][start:start + rows].astype(jnp.float32)
        inner = (jnp.where(mine, inner, 0.0) * low_rank_scale).astype(jnp.bfloat16)
        for which in range(2):
            column = 0
            for n, width in enumerate(widths):
                factor = ups[e][0, which, :, column:column + width]
                low = jnp.dot(inner, jnp.concatenate([factor, factor], axis=0), preferred_element_type=jnp.float32)
                term = parts[which * len(widths) + n][e * rows:(e + 1) * rows].astype(jnp.float32) + low
                out_ref[0, which, e, :, column:column + width] = term.astype(jnp.bfloat16)
                column += width


def add_low_rank(parts, inner, start, rows, first, count, up_pool, table, each, hint=1 << 10):
    columns = up_pool.shape[3]
    rank = up_pool.shape[2]
    widths = [part.shape[1] for part in parts[:len(parts) // 2]]

    def up_spec(e):
        return pl.BlockSpec((1, 2, rank, columns), lambda n, tab: (tab[0, (first + n) * each + e], 0, 0, 0))

    return pl.pallas_call(
        functools.partial(low_rank_kernel, first, each, start, widths),
        out_shape=jax.ShapeDtypeStruct((count, 2, each, rows, columns), jnp.bfloat16),
        grid_spec=pltpu.PrefetchScalarGridSpec(
            num_scalar_prefetch=1,
            grid=(count,),
            in_specs=[pl.BlockSpec(inner.shape, lambda n, tab: (0, 0, 0))]
            + [pl.BlockSpec((each * rows, part.shape[1]), lambda n, tab: (first + n, 0)) for part in parts]
            + [up_spec(e) for e in range(each)],
            out_specs=pl.BlockSpec((1, 2, each, rows, columns), lambda n, tab: (n, 0, 0, 0, 0)),
        ),
        compiler_params=pltpu.CompilerParams(vmem_limit_bytes=24 << 20),
        cost_estimate=pl.CostEstimate(flops=hint, bytes_accessed=1 << 10, transcendentals=0),
    )(table, inner, *parts, *([up_pool] * each))


def add(x, y):
    return (x.astype(jnp.float32) + y.astype(jnp.float32)).astype(x.dtype)


def hop_pairs(level, nseq):
    return [(level, level + 1), (nseq - 1 - level, nseq - 2 - level)]


def scatter_line(own, first, nseq):
    last = nseq - 2
    arrived = {(0, slot): hop for slot, hop in enumerate(first)}
    for step in range(nseq - 1):
        for level in range(1, step + 1):
            slot = step - level if level < nseq // 2 else step
            send = add(own[slot], arrived[level - 1, step - 1])
            arrived[level, step] = lax.ppermute(send, "seq", hop_pairs(level, nseq))
    total = own[nseq - 1].astype(jnp.float32)
    for level in range(nseq - 1):
        total = total + arrived[level, last].astype(jnp.float32)
    return total


def after(x, gate):
    return lax.optimization_barrier((x, gate))[0]


def shards(tokens, gate_weight, up_weight, down_pool, up_pool, req_len, req_adapter, owner_slot):
    nseq = lax.axis_size("seq")
    ntp = lax.axis_size("tp")
    each = ntp // nseq
    me = lax.axis_index("tp")
    place = jnp.arange(ntp, dtype=jnp.int32)
    ordered = chunk_of(place // each, nseq) * each + place % each
    position = jnp.sum(jnp.where(ordered[:, None] == place[None, :], place[:, None], 0), axis=0)
    down_slot, down_here = held(
        slots_of(place, req_len, req_adapter, owner_slot), me * down_pool.shape[0], down_pool.shape[0]
    )
    up_slot, up_here = held(
        slots_of(ordered, req_len, req_adapter, owner_slot),
        lax.axis_index("seq") * up_pool.shape[0],
        up_pool.shape[0],
    )
    down_table = jnp.stack([down_slot, down_here, jnp.full_like(down_slot, me), position])
    up_table = jnp.stack([up_slot, up_here, ordered])
    columns = gate_weight.shape[1]
    tile = 256 if columns % 256 == 0 else 128
    tiles = columns // tile
    first, second = GROUPS
    rows = first[0]

    pieces = gather_rows(tokens[:rows], ntp)
    (x,), mine = assemble(pieces, first, down_pool, down_table, 1 << 20)
    x = x.reshape(-1, x.shape[2])
    cuts = [(w, f, c) for w in (gate_weight, up_weight) for f, c in ((0, tiles // 2), (tiles // 2, tiles - tiles // 2))]
    left = list(cuts)

    def piece(gate):
        if not left:
            return None
        weight, begin, count = left.pop(0)
        return project(after(x, gate), weight, begin, count, tile)

    shared, parts = sum_beside(mine.reshape(-1, mine.shape[2]), "tp", ntp, piece)
    pieces = gather_rows(after(tokens[rows:], shared), ntp)
    inner, more = sum_beside(shared, "seq", nseq, piece)
    parts = [part for part in parts + more if part is not None]
    inner = inner.reshape(mine.shape)

    def terms(parts, inner, start, rows, first, count, gate, hint=1 << 10):
        given = after(inner, gate) if gate is not None else inner
        return add_low_rank(parts, given, start, rows, first, count, up_pool, up_table, each, hint)

    def first_hop(send):
        return lax.ppermute(send, "seq", hop_pairs(0, nseq))

    head = terms(parts, inner, 0, rows, 0, 1, None)
    pieces = list(after(tuple(pieces), head))
    (x,), mine = assemble(pieces, second, down_pool, down_table, AHEAD)
    head_hop = first_hop(head)
    shared, _ = sum_beside(mine.reshape(-1, mine.shape[2]), "tp", ntp, lambda gate: None)
    rest = terms(parts, inner, 0, rows, 1, nseq - 2, shared)
    rest_hop = first_hop(rest)
    kept = terms(parts, inner, 0, rows, nseq - 1, 1, rest)
    inner = sum_one_step(shared, "seq", nseq).reshape(mine.shape)
    x = after(x.reshape(-1, x.shape[2]), (head_hop, kept))
    own = [head[0]] + [rest[slot] for slot in range(nseq - 2)] + [kept[0]]

    rows = second[0]
    parts = [project(x, weight, 0, tiles, tile, AHEAD) for weight in (gate_weight, up_weight)]
    sent = [terms(parts, inner, 0, rows, 0, 1, None)]
    for slot in range(1, nseq):
        sent.append(terms(parts, inner, 0, rows, slot, 1, sent[-1]))
    head_hop = after(head_hop, sent[0])
    rest_hop = after(rest_hop, sent[-1])
    hops = []
    for slot in range(nseq - 1):
        hops.append(first_hop(after(sent[slot], hops[slot - 2] if slot > 1 else rest_hop)))

    totals = [
        scatter_line(own, [head_hop[0]] + [rest_hop[slot] for slot in range(nseq - 2)], nseq),
        scatter_line([term[0] for term in sent], [hop[0] for hop in hops], nseq),
    ]
    out = [(jax.nn.silu(total[0]) * total[1]).astype(jnp.bfloat16) for total in totals]
    return jnp.concatenate(out, axis=1).reshape(-1, columns)


def solution(mesh):
    placed = (
        P("tp", "seq"),
        P("seq", "tp"),
        P("seq", "tp"),
        P("tp", None, "seq"),
        P("seq", None, None, "tp"),
        P(),
        P(),
        P(),
    )
    return jax.shard_map(
        shards, mesh=mesh, in_specs=placed, out_specs=P("seq", "tp"), check_vma=False
    )
```

```python
import functools

import jax
import jax.numpy as jnp
from jax import lax
from jax.experimental import pallas as pl
from jax.experimental.pallas import tpu as pltpu
from jax.sharding import PartitionSpec as P

SEG_ROWS = 128
GROUPS = ((48,), (80,))
AHEAD = 1 << 36

low_rank_scale = 0.5


def slots_of(segment, req_len, req_adapter, owner_slot):
    order = jnp.arange(req_len.shape[0], dtype=jnp.int32)
    ends = jnp.sum(jnp.where(order[:, None] <= order[None, :], req_len[:, None], 0), axis=0)
    seg_request = jnp.sum((ends[None, :] <= segment[:, None]).astype(jnp.int32), axis=1)
    adapter = jnp.sum(jnp.where(seg_request[:, None] == order[None, :], req_adapter[None, :], 0), axis=1)
    ids = jnp.arange(owner_slot.shape[0], dtype=jnp.int32)
    return jnp.sum(jnp.where(adapter[:, None] == ids[None, :], owner_slot[None, :], 0), axis=1)


def chunk_of(slot, nseq):
    me = lax.axis_index("seq")
    half = me < nseq // 2
    far = jnp.where(half, nseq - 1 - me, me)
    near = slot - far
    far_chunk = jnp.where(half, nseq - 1 - slot, slot)
    near_chunk = jnp.where(half, near, nseq - 1 - near)
    chunk = jnp.where(slot < far, far_chunk, near_chunk)
    return jnp.where(slot == nseq - 1, me, chunk)


def held(seg_slot, first, count):
    local = seg_slot - first
    here = (local >= 0) & (local < count)
    return jnp.clip(local, 0, count - 1), here.astype(jnp.int32)


def swap(x, axis, size, mask):
    return lax.ppermute(x, axis, [(i, i ^ mask) for i in range(size)])


def gather_chips(x, ntp):
    return [x] + [swap(x, "tp", ntp, 2 * m) for m in range(1, ntp // 2)]


def gather_cores(chips, ntp):
    pieces = []
    for piece in chips:
        pieces += [piece, swap(piece, "tp", ntp, 1)]
    return pieces


def sum_one_step(x, axis, size):
    parts = [lax.ppermute(x, axis, [(i, (i + k) % size) for i in range(size)]) for k in range(1, size)]
    total = x.astype(jnp.float32)
    for part in parts:
        total = total + part.astype(jnp.float32)
    return total.astype(x.dtype)


def sum_beside(x, axis, size, beside):
    done = []
    mask = 1
    while mask < size:
        other = swap(x, axis, size, mask)
        if mask > 1 or axis != "tp":
            done.append(beside(x))
            other = after(other, done[-1]) if done[-1] is not None else other
        x = add(x, other)
        mask *= 2
    return x, done


def assemble_kernel(segs, group, tab_ref, *refs):
    pieces, down_ref, xs, inner_ref = refs[:segs], refs[segs], refs[segs + 1:-1], refs[-1]
    me = tab_ref[2, 0]
    for n, piece in enumerate(pieces):
        start = 0
        for x_ref, rows in zip(xs, group):
            x_ref[tab_ref[3, me ^ n]] = piece[start:start + rows]
            start += rows
    start = 0
    for x_ref, rows in zip(xs, group):
        for pair in range(segs // 2):
            halves = []
            for k in (2 * pair, 2 * pair + 1):
                product = lax.dot_general(
                    x_ref[tab_ref[3, k]],
                    down_ref[tab_ref[0, k]],
                    (((1,), (1,)), ((), ())),
                    preferred_element_type=jnp.float32,
                )
                halves.append(product * tab_ref[1, k].astype(jnp.float32))
            inner_ref[pair, start:start + rows] = jnp.concatenate(halves, axis=1).astype(jnp.bfloat16)
        start += rows


def assemble(pieces, group, down_pool, table, hint):
    segs = len(pieces)
    total, width = pieces[0].shape
    rank = down_pool.shape[1]
    vmem = pl.BlockSpec(memory_space=pltpu.VMEM)
    *xs, mine = pl.pallas_call(
        functools.partial(assemble_kernel, segs, group),
        out_shape=[jax.ShapeDtypeStruct((segs, rows, width), jnp.bfloat16) for rows in group]
        + [jax.ShapeDtypeStruct((segs // 2, total, 2 * rank), jnp.bfloat16)],
        in_specs=[pl.BlockSpec(memory_space=pltpu.SMEM)] + [vmem] * (segs + 1),
        out_specs=[vmem] * (len(group) + 1),
        compiler_params=pltpu.CompilerParams(vmem_limit_bytes=12 << 20),
        cost_estimate=pl.CostEstimate(flops=hint, bytes_accessed=4 * segs * total * width, transcendentals=0),
    )(table, *pieces, down_pool)
    return xs, mine


def project_kernel(x_ref, weight_ref, out_ref):
    out_ref[...] = jnp.dot(x_ref[...], weight_ref[...], preferred_element_type=jnp.float32).astype(jnp.bfloat16)


def project(x, weight, first, count, tile, hint=0):
    width = weight.shape[0]
    rows = x.shape[0]
    return pl.pallas_call(
        project_kernel,
        out_shape=jax.ShapeDtypeStruct((rows, count * tile), jnp.bfloat16),
        grid=(count,),
        in_specs=[
            pl.BlockSpec((rows, width), lambda n: (0, 0)),
            pl.BlockSpec((width, tile), lambda n: (0, first + n)),
        ],
        out_specs=pl.BlockSpec((rows, tile), lambda n: (0, n)),
        compiler_params=pltpu.CompilerParams(vmem_limit_bytes=16 << 20),
        cost_estimate=pl.CostEstimate(
            flops=hint or 2 * rows * width * count * tile, bytes_accessed=2 * width * count * tile, transcendentals=0
        ),
    )(x, weight)


def low_rank_kernel(first, each, start, widths, tab_ref, inner_ref, *refs):
    parts, ups, out_ref = refs[:2 * len(widths)], refs[2 * len(widths):-1], refs[-1]
    slot = first + pl.program_id(0)
    lanes = inner_ref.shape[2]
    rank = lanes // 2
    rows = out_ref.shape[3]
    lane = lax.broadcasted_iota(jnp.int32, (rows, lanes), 1)
    for e in range(each):
        seg = tab_ref[2, slot * each + e]
        mine = (lane // rank == seg % 2) & (tab_ref[1, slot * each + e] == 1)
        inner = inner_ref[seg // 2][start:start + rows].astype(jnp.float32)
        inner = (jnp.where(mine, inner, 0.0) * low_rank_scale).astype(jnp.bfloat16)
        for which in range(2):
            column = 0
            for n, width in enumerate(widths):
                factor = ups[e][0, which, :, column:column + width]
                low = jnp.dot(inner, jnp.concatenate([factor, factor], axis=0), preferred_element_type=jnp.float32)
                term = parts[which * len(widths) + n][e * rows:(e + 1) * rows].astype(jnp.float32) + low
                out_ref[0, which, e, :, column:column + width] = term.astype(jnp.bfloat16)
                column += width


def add_low_rank(parts, inner, start, rows, first, count, up_pool, table, each, hint=1 << 10):
    columns = up_pool.shape[3]
    rank = up_pool.shape[2]
    widths = [part.shape[1] for part in parts[:len(parts) // 2]]

    def up_spec(e):
        return pl.BlockSpec((1, 2, rank, columns), lambda n, tab: (tab[0, (first + n) * each + e], 0, 0, 0))

    return pl.pallas_call(
        functools.partial(low_rank_kernel, first, each, start, widths),
        out_shape=jax.ShapeDtypeStruct((count, 2, each, rows, columns), jnp.bfloat16),
        grid_spec=pltpu.PrefetchScalarGridSpec(
            num_scalar_prefetch=1,
            grid=(count,),
            in_specs=[pl.BlockSpec(inner.shape, lambda n, tab: (0, 0, 0))]
            + [pl.BlockSpec((each * rows, part.shape[1]), lambda n, tab: (first + n, 0)) for part in parts]
            + [up_spec(e) for e in range(each)],
            out_specs=pl.BlockSpec((1, 2, each, rows, columns), lambda n, tab: (n, 0, 0, 0, 0)),
        ),
        compiler_params=pltpu.CompilerParams(vmem_limit_bytes=24 << 20),
        cost_estimate=pl.CostEstimate(flops=hint, bytes_accessed=1 << 10, transcendentals=0),
    )(table, inner, *parts, *([up_pool] * each))


def add(x, y):
    return (x.astype(jnp.float32) + y.astype(jnp.float32)).astype(x.dtype)


def hop_pairs(level, nseq):
    return [(level, level + 1), (nseq - 1 - level, nseq - 2 - level)]


def scatter_line(own, first, nseq, given=None):
    last = nseq - 2
    arrived = {(0, slot): hop for slot, hop in enumerate(first)}
    arrived.update(given or {})
    for step in range(nseq - 1):
        for level in range(1, step + 1):
            if (level, step) in arrived:
                continue
            slot = step - level if level < nseq // 2 else step
            send = add(own[slot], arrived[level - 1, step - 1])
            arrived[level, step] = lax.ppermute(send, "seq", hop_pairs(level, nseq))
    total = own[nseq - 1].astype(jnp.float32)
    for level in range(nseq - 1):
        total = total + arrived[level, last].astype(jnp.float32)
    return total


def after(x, gate):
    return lax.optimization_barrier((x, gate))[0]


def shards(tokens, gate_weight, up_weight, down_pool, up_pool, req_len, req_adapter, owner_slot):
    nseq = lax.axis_size("seq")
    ntp = lax.axis_size("tp")
    each = ntp // nseq
    me = lax.axis_index("tp")
    place = jnp.arange(ntp, dtype=jnp.int32)
    ordered = chunk_of(place // each, nseq) * each + place % each
    position = jnp.sum(jnp.where(ordered[:, None] == place[None, :], place[:, None], 0), axis=0)
    down_slot, down_here = held(
        slots_of(place, req_len, req_adapter, owner_slot), me * down_pool.shape[0], down_pool.shape[0]
    )
    up_slot, up_here = held(
        slots_of(ordered, req_len, req_adapter, owner_slot),
        lax.axis_index("seq") * up_pool.shape[0],
        up_pool.shape[0],
    )
    down_table = jnp.stack([down_slot, down_here, jnp.full_like(down_slot, me), position])
    up_table = jnp.stack([up_slot, up_here, ordered])
    columns = gate_weight.shape[1]
    tile = 256 if columns % 256 == 0 else 128
    tiles = columns // tile
    (first,), (later,) = GROUPS
    rows = first

    pieces = gather_cores(gather_chips(tokens[:rows], ntp), ntp)
    (x,), mine = assemble(pieces, (first,), down_pool, down_table, 1 << 20)
    x = x.reshape(-1, x.shape[2])
    cuts = [(w, f, c) for w in (gate_weight, up_weight) for f, c in ((0, tiles // 2), (tiles // 2, tiles - tiles // 2))]
    left = list(cuts)

    def piece(gate):
        if not left:
            return None
        weight, begin, count = left.pop(0)
        return project(after(x, gate), weight, begin, count, tile)

    shared, parts = sum_beside(mine.reshape(-1, mine.shape[2]), "tp", ntp, piece)
    chips = gather_chips(after(tokens[rows:], shared), ntp)
    inner, more = sum_beside(shared, "seq", nseq, piece)
    parts = [part for part in parts + more if part is not None]
    inner = inner.reshape(mine.shape)

    def terms(parts, inner, start, rows, first, count, gate, hint=1 << 10):
        given = after(inner, gate) if gate is not None else inner
        return add_low_rank(parts, given, start, rows, first, count, up_pool, up_table, each, hint)

    def first_hop(send):
        return lax.ppermute(send, "seq", hop_pairs(0, nseq))

    head = terms(parts, inner, 0, rows, 0, 1, None)
    pieces = gather_cores(list(after(tuple(chips), head)), ntp)
    (x,), mine = assemble(pieces, (later,), down_pool, down_table, AHEAD)
    head_hop = first_hop(head)
    shared, _ = sum_beside(mine.reshape(-1, mine.shape[2]), "tp", ntp, lambda gate: None)
    rest = terms(parts, inner, 0, rows, 1, nseq - 2, shared)
    rest_hop = first_hop(rest)
    kept = terms(parts, inner, 0, rows, nseq - 1, 1, rest)
    inner = sum_one_step(shared, "seq", nseq).reshape(mine.shape)
    second = add(head[0], after(head_hop, rest)[0])
    second_hop = lax.ppermute(second, "seq", hop_pairs(1, nseq))
    x = after(x.reshape(-1, x.shape[2]), (second, kept))
    own = [head[0]] + [rest[slot] for slot in range(nseq - 2)] + [kept[0]]

    rows = later
    parts = [project(x, weight, 0, tiles, tile, AHEAD) for weight in (gate_weight, up_weight)]
    sent = [terms(parts, inner, 0, rows, 0, 1, None)]
    for slot in range(1, nseq):
        sent.append(terms(parts, inner, 0, rows, slot, 1, (sent[-1], second_hop)))
    rest_hop = after(rest_hop, sent[-1])
    hops = []
    for slot in range(nseq - 1):
        hops.append(first_hop(after(sent[slot], hops[slot - 2] if slot > 1 else rest_hop)))

    totals = [
        scatter_line(own, [head_hop[0]] + [rest_hop[slot] for slot in range(nseq - 2)], nseq, {(1, 1): second_hop}),
        scatter_line([term[0] for term in sent], [hop[0] for hop in hops], nseq),
    ]
    out = [(jax.nn.silu(total[0]) * total[1]).astype(jnp.bfloat16) for total in totals]
    return jnp.concatenate(out, axis=1).reshape(-1, columns)


def solution(mesh):
    placed = (
        P("tp", "seq"),
        P("seq", "tp"),
        P("seq", "tp"),
        P("tp", None, "seq"),
        P("seq", None, None, "tp"),
        P(),
        P(),
        P(),
    )
    return jax.shard_map(
        shards, mesh=mesh, in_specs=placed, out_specs=P("seq", "tp"), check_vma=False
    )
```

```python
import functools

import jax
import jax.numpy as jnp
from jax import lax
from jax.experimental import pallas as pl
from jax.experimental.pallas import tpu as pltpu
from jax.sharding import PartitionSpec as P

SEG_ROWS = 128
GROUPS = ((48,), (80,))
AHEAD = 1 << 36

low_rank_scale = 0.5


def slots_of(segment, req_len, req_adapter, owner_slot):
    order = jnp.arange(req_len.shape[0], dtype=jnp.int32)
    ends = jnp.sum(jnp.where(order[:, None] <= order[None, :], req_len[:, None], 0), axis=0)
    seg_request = jnp.sum((ends[None, :] <= segment[:, None]).astype(jnp.int32), axis=1)
    adapter = jnp.sum(jnp.where(seg_request[:, None] == order[None, :], req_adapter[None, :], 0), axis=1)
    ids = jnp.arange(owner_slot.shape[0], dtype=jnp.int32)
    return jnp.sum(jnp.where(adapter[:, None] == ids[None, :], owner_slot[None, :], 0), axis=1)


def chunk_of(slot, nseq):
    me = lax.axis_index("seq")
    half = me < nseq // 2
    far = jnp.where(half, nseq - 1 - me, me)
    near = slot - far
    far_chunk = jnp.where(half, nseq - 1 - slot, slot)
    near_chunk = jnp.where(half, near, nseq - 1 - near)
    chunk = jnp.where(slot < far, far_chunk, near_chunk)
    return jnp.where(slot == nseq - 1, me, chunk)


def held(seg_slot, first, count):
    local = seg_slot - first
    here = (local >= 0) & (local < count)
    return jnp.clip(local, 0, count - 1), here.astype(jnp.int32)


def swap(x, axis, size, mask):
    return lax.ppermute(x, axis, [(i, i ^ mask) for i in range(size)])


def gather_chips(x, ntp):
    return [x] + [swap(x, "tp", ntp, 2 * m) for m in range(1, ntp // 2)]


def gather_cores(chips, ntp):
    pieces = []
    for piece in chips:
        pieces += [piece, swap(piece, "tp", ntp, 1)]
    return pieces


def sum_one_step(x, axis, size):
    parts = [lax.ppermute(x, axis, [(i, (i + k) % size) for i in range(size)]) for k in range(1, size)]
    total = x.astype(jnp.float32)
    for part in parts:
        total = total + part.astype(jnp.float32)
    return total.astype(x.dtype)


def sum_beside(x, axis, size, beside):
    done = []
    mask = 1
    while mask < size:
        other = swap(x, axis, size, mask)
        if mask > 1 or axis != "tp":
            done.append(beside(x))
            other = after(other, done[-1]) if done[-1] is not None else other
        x = add(x, other)
        mask *= 2
    return x, done


def assemble_kernel(segs, group, tab_ref, *refs):
    pieces, down_ref, xs, inner_ref = refs[:segs], refs[segs], refs[segs + 1:-1], refs[-1]
    me = tab_ref[2, 0]
    for n, piece in enumerate(pieces):
        start = 0
        for x_ref, rows in zip(xs, group):
            x_ref[tab_ref[3, me ^ n]] = piece[start:start + rows]
            start += rows
    start = 0
    for x_ref, rows in zip(xs, group):
        for pair in range(segs // 2):
            halves = []
            for k in (2 * pair, 2 * pair + 1):
                product = lax.dot_general(
                    x_ref[tab_ref[3, k]],
                    down_ref[tab_ref[0, k]],
                    (((1,), (1,)), ((), ())),
                    preferred_element_type=jnp.float32,
                )
                halves.append(product * tab_ref[1, k].astype(jnp.float32))
            inner_ref[pair, start:start + rows] = jnp.concatenate(halves, axis=1).astype(jnp.bfloat16)
        start += rows


def assemble(pieces, group, down_pool, table, hint):
    segs = len(pieces)
    total, width = pieces[0].shape
    rank = down_pool.shape[1]
    vmem = pl.BlockSpec(memory_space=pltpu.VMEM)
    *xs, mine = pl.pallas_call(
        functools.partial(assemble_kernel, segs, group),
        out_shape=[jax.ShapeDtypeStruct((segs, rows, width), jnp.bfloat16) for rows in group]
        + [jax.ShapeDtypeStruct((segs // 2, total, 2 * rank), jnp.bfloat16)],
        in_specs=[pl.BlockSpec(memory_space=pltpu.SMEM)] + [vmem] * (segs + 1),
        out_specs=[vmem] * (len(group) + 1),
        compiler_params=pltpu.CompilerParams(vmem_limit_bytes=12 << 20),
        cost_estimate=pl.CostEstimate(flops=hint, bytes_accessed=4 * segs * total * width, transcendentals=0),
    )(table, *pieces, down_pool)
    return xs, mine


def project_kernel(x_ref, weight_ref, out_ref):
    out_ref[...] = jnp.dot(x_ref[...], weight_ref[...], preferred_element_type=jnp.float32).astype(jnp.bfloat16)


def project(x, weight, first, count, tile, hint=0):
    width = weight.shape[0]
    rows = x.shape[0]
    return pl.pallas_call(
        project_kernel,
        out_shape=jax.ShapeDtypeStruct((rows, count * tile), jnp.bfloat16),
        grid=(count,),
        in_specs=[
            pl.BlockSpec((rows, width), lambda n: (0, 0)),
            pl.BlockSpec((width, tile), lambda n: (0, first + n)),
        ],
        out_specs=pl.BlockSpec((rows, tile), lambda n: (0, n)),
        compiler_params=pltpu.CompilerParams(vmem_limit_bytes=16 << 20),
        cost_estimate=pl.CostEstimate(
            flops=hint or 2 * rows * width * count * tile, bytes_accessed=2 * width * count * tile, transcendentals=0
        ),
    )(x, weight)


def low_rank_kernel(first, each, start, widths, tab_ref, inner_ref, *refs):
    parts, ups, out_ref = refs[:2 * len(widths)], refs[2 * len(widths):-1], refs[-1]
    slot = first + pl.program_id(0)
    lanes = inner_ref.shape[2]
    rank = lanes // 2
    rows = out_ref.shape[3]
    lane = lax.broadcasted_iota(jnp.int32, (rows, lanes), 1)
    for e in range(each):
        seg = tab_ref[2, slot * each + e]
        mine = (lane // rank == seg % 2) & (tab_ref[1, slot * each + e] == 1)
        inner = inner_ref[seg // 2][start:start + rows].astype(jnp.float32)
        inner = (jnp.where(mine, inner, 0.0) * low_rank_scale).astype(jnp.bfloat16)
        for which in range(2):
            column = 0
            for n, width in enumerate(widths):
                factor = ups[e][0, which, :, column:column + width]
                low = jnp.dot(inner, jnp.concatenate([factor, factor], axis=0), preferred_element_type=jnp.float32)
                term = parts[which * len(widths) + n][e * rows:(e + 1) * rows].astype(jnp.float32) + low
                out_ref[0, which, e, :, column:column + width] = term.astype(jnp.bfloat16)
                column += width


def add_low_rank(parts, inner, start, rows, first, count, up_pool, table, each, hint=1 << 10):
    columns = up_pool.shape[3]
    rank = up_pool.shape[2]
    widths = [part.shape[1] for part in parts[:len(parts) // 2]]

    def up_spec(e):
        return pl.BlockSpec((1, 2, rank, columns), lambda n, tab: (tab[0, (first + n) * each + e], 0, 0, 0))

    return pl.pallas_call(
        functools.partial(low_rank_kernel, first, each, start, widths),
        out_shape=jax.ShapeDtypeStruct((count, 2, each, rows, columns), jnp.bfloat16),
        grid_spec=pltpu.PrefetchScalarGridSpec(
            num_scalar_prefetch=1,
            grid=(count,),
            in_specs=[pl.BlockSpec(inner.shape, lambda n, tab: (0, 0, 0))]
            + [pl.BlockSpec((each * rows, part.shape[1]), lambda n, tab: (first + n, 0)) for part in parts]
            + [up_spec(e) for e in range(each)],
            out_specs=pl.BlockSpec((1, 2, each, rows, columns), lambda n, tab: (n, 0, 0, 0, 0)),
        ),
        compiler_params=pltpu.CompilerParams(vmem_limit_bytes=24 << 20),
        cost_estimate=pl.CostEstimate(flops=hint, bytes_accessed=1 << 10, transcendentals=0),
    )(table, inner, *parts, *([up_pool] * each))


def add(x, y):
    return (x.astype(jnp.float32) + y.astype(jnp.float32)).astype(x.dtype)


def hop_pairs(level, nseq):
    return [(level, level + 1), (nseq - 1 - level, nseq - 2 - level)]


def scatter_line(own, first, nseq, given=None):
    last = nseq - 2
    arrived = {(0, slot): hop for slot, hop in enumerate(first)}
    arrived.update(given or {})
    for step in range(nseq - 1):
        for level in range(1, step + 1):
            if (level, step) in arrived:
                continue
            slot = step - level if level < nseq // 2 else step
            send = add(own[slot], arrived[level - 1, step - 1])
            arrived[level, step] = lax.ppermute(send, "seq", hop_pairs(level, nseq))
    total = own[nseq - 1].astype(jnp.float32)
    for level in range(nseq - 1):
        total = total + arrived[level, last].astype(jnp.float32)
    return total


def after(x, gate):
    return lax.optimization_barrier((x, gate))[0]


def shards(tokens, gate_weight, up_weight, down_pool, up_pool, req_len, req_adapter, owner_slot):
    nseq = lax.axis_size("seq")
    ntp = lax.axis_size("tp")
    each = ntp // nseq
    me = lax.axis_index("tp")
    place = jnp.arange(ntp, dtype=jnp.int32)
    ordered = chunk_of(place // each, nseq) * each + place % each
    position = jnp.sum(jnp.where(ordered[:, None] == place[None, :], place[:, None], 0), axis=0)
    down_slot, down_here = held(
        slots_of(place, req_len, req_adapter, owner_slot), me * down_pool.shape[0], down_pool.shape[0]
    )
    up_slot, up_here = held(
        slots_of(ordered, req_len, req_adapter, owner_slot),
        lax.axis_index("seq") * up_pool.shape[0],
        up_pool.shape[0],
    )
    down_table = jnp.stack([down_slot, down_here, jnp.full_like(down_slot, me), position])
    up_table = jnp.stack([up_slot, up_here, ordered])
    columns = gate_weight.shape[1]
    tile = 256 if columns % 256 == 0 else 128
    tiles = columns // tile
    (first,), (later,) = GROUPS
    rows = first

    pieces = gather_cores(gather_chips(tokens[:rows], ntp), ntp)
    (x,), mine = assemble(pieces, (first,), down_pool, down_table, 1 << 20)
    x = x.reshape(-1, x.shape[2])
    cuts = [(w, f, c) for w in (gate_weight, up_weight) for f, c in ((0, tiles // 2), (tiles // 2, tiles - tiles // 2))]
    left = list(cuts)

    def piece(gate):
        if not left:
            return None
        weight, begin, count = left.pop(0)
        return project(after(x, gate), weight, begin, count, tile)

    shared, parts = sum_beside(mine.reshape(-1, mine.shape[2]), "tp", ntp, piece)
    chips = gather_chips(after(tokens[rows:], shared), ntp)
    inner, more = sum_beside(shared, "seq", nseq, piece)
    parts = [part for part in parts + more if part is not None]
    inner = inner.reshape(mine.shape)

    def terms(parts, inner, start, rows, first, count, gate, hint=1 << 10):
        given = after(inner, gate) if gate is not None else inner
        return add_low_rank(parts, given, start, rows, first, count, up_pool, up_table, each, hint)

    def first_hop(send):
        return lax.ppermute(send, "seq", hop_pairs(0, nseq))

    head = terms(parts, inner, 0, rows, 0, 1, None)
    pieces = gather_cores(list(after(tuple(chips), head)), ntp)
    (x,), mine = assemble(pieces, (later,), down_pool, down_table, AHEAD)
    head_hop = first_hop(head)
    shared, _ = sum_beside(mine.reshape(-1, mine.shape[2]), "tp", ntp, lambda gate: None)
    rest = terms(parts, inner, 0, rows, 1, nseq - 2, shared)
    rest_hop = first_hop(rest)
    kept = terms(parts, inner, 0, rows, nseq - 1, 1, rest)
    inner = sum_one_step(shared, "seq", nseq).reshape(mine.shape)
    second = add(head[0], after(head_hop, rest)[0])
    second_hop = lax.ppermute(second, "seq", hop_pairs(1, nseq))
    x = after(x.reshape(-1, x.shape[2]), (second, kept))
    own = [head[0]] + [rest[slot] for slot in range(nseq - 2)] + [kept[0]]

    rows = later
    parts = [project(x, weight, 0, tiles, tile, AHEAD) for weight in (gate_weight, up_weight)]
    sent = [terms(parts, inner, 0, rows, 0, 1, None)]
    for slot in range(1, nseq):
        sent.append(terms(parts, inner, 0, rows, slot, 1, (sent[-1], second_hop)))
    rest_hop = after(rest_hop, sent[-1])
    third_hop = lax.ppermute(add(rest[0], rest_hop[0]), "seq", hop_pairs(1, nseq))
    hops = []
    for slot in range(nseq - 1):
        hops.append(first_hop(after(sent[slot], hops[slot - 2] if slot > 1 else rest_hop)))

    hops[0] = after(hops[0], third_hop)
    totals = [
        scatter_line(own, [head_hop[0]] + [rest_hop[slot] for slot in range(nseq - 2)], nseq, {(1, 1): second_hop, (1, 2): third_hop}),
        scatter_line([term[0] for term in sent], [hop[0] for hop in hops], nseq),
    ]
    out = [(jax.nn.silu(total[0]) * total[1]).astype(jnp.bfloat16) for total in totals]
    return jnp.concatenate(out, axis=1).reshape(-1, columns)


def solution(mesh):
    placed = (
        P("tp", "seq"),
        P("seq", "tp"),
        P("seq", "tp"),
        P("tp", None, "seq"),
        P("seq", None, None, "tp"),
        P(),
        P(),
        P(),
    )
    return jax.shard_map(
        shards, mesh=mesh, in_specs=placed, out_specs=P("seq", "tp"), check_vma=False
    )
```

```python
import functools

import jax
import jax.numpy as jnp
from jax import lax
from jax.experimental import pallas as pl
from jax.experimental.pallas import tpu as pltpu
from jax.sharding import PartitionSpec as P

SEG_ROWS = 128
GROUPS = ((48,), (80,))
AHEAD = 1 << 36

low_rank_scale = 0.5


def slots_of(segment, req_len, req_adapter, owner_slot):
    order = jnp.arange(req_len.shape[0], dtype=jnp.int32)
    ends = jnp.sum(jnp.where(order[:, None] <= order[None, :], req_len[:, None], 0), axis=0)
    seg_request = jnp.sum((ends[None, :] <= segment[:, None]).astype(jnp.int32), axis=1)
    adapter = jnp.sum(jnp.where(seg_request[:, None] == order[None, :], req_adapter[None, :], 0), axis=1)
    ids = jnp.arange(owner_slot.shape[0], dtype=jnp.int32)
    return jnp.sum(jnp.where(adapter[:, None] == ids[None, :], owner_slot[None, :], 0), axis=1)


def chunk_of(slot, nseq):
    me = lax.axis_index("seq")
    half = me < nseq // 2
    far = jnp.where(half, nseq - 1 - me, me)
    near = slot - far
    far_chunk = jnp.where(half, nseq - 1 - slot, slot)
    near_chunk = jnp.where(half, near, nseq - 1 - near)
    chunk = jnp.where(slot < far, far_chunk, near_chunk)
    return jnp.where(slot == nseq - 1, me, chunk)


def held(seg_slot, first, count):
    local = seg_slot - first
    here = (local >= 0) & (local < count)
    return jnp.clip(local, 0, count - 1), here.astype(jnp.int32)


def swap(x, axis, size, mask):
    return lax.ppermute(x, axis, [(i, i ^ mask) for i in range(size)])


def gather_chips(x, ntp):
    return [x] + [swap(x, "tp", ntp, 2 * m) for m in range(1, ntp // 2)]


def gather_cores(chips, ntp):
    pieces = []
    for piece in chips:
        pieces += [piece, swap(piece, "tp", ntp, 1)]
    return pieces


def sum_one_step(x, axis, size):
    parts = [lax.ppermute(x, axis, [(i, (i + k) % size) for i in range(size)]) for k in range(1, size)]
    total = x.astype(jnp.float32)
    for part in parts:
        total = total + part.astype(jnp.float32)
    return total.astype(x.dtype)


def sum_beside(x, axis, size, beside):
    done = []
    steps = [x]
    mask = 1
    while mask < size:
        other = swap(x, axis, size, mask)
        if mask > 1 or axis != "tp":
            done.append(beside(x))
            other = after(other, done[-1]) if done[-1] is not None else other
        x = add(x, other)
        steps.append(x)
        mask *= 2
    return steps, done


def assemble_kernel(segs, group, tab_ref, *refs):
    pieces, down_ref, xs, inner_ref = refs[:segs], refs[segs], refs[segs + 1:-1], refs[-1]
    me = tab_ref[2, 0]
    for n, piece in enumerate(pieces):
        start = 0
        for x_ref, rows in zip(xs, group):
            x_ref[tab_ref[3, me ^ n]] = piece[start:start + rows]
            start += rows
    start = 0
    for x_ref, rows in zip(xs, group):
        for pair in range(segs // 2):
            halves = []
            for k in (2 * pair, 2 * pair + 1):
                product = lax.dot_general(
                    x_ref[tab_ref[3, k]],
                    down_ref[tab_ref[0, k]],
                    (((1,), (1,)), ((), ())),
                    preferred_element_type=jnp.float32,
                )
                halves.append(product * tab_ref[1, k].astype(jnp.float32))
            inner_ref[pair, start:start + rows] = jnp.concatenate(halves, axis=1).astype(jnp.bfloat16)
        start += rows


def assemble(pieces, group, down_pool, table, hint):
    segs = len(pieces)
    total, width = pieces[0].shape
    rank = down_pool.shape[1]
    vmem = pl.BlockSpec(memory_space=pltpu.VMEM)
    *xs, mine = pl.pallas_call(
        functools.partial(assemble_kernel, segs, group),
        out_shape=[jax.ShapeDtypeStruct((segs, rows, width), jnp.bfloat16) for rows in group]
        + [jax.ShapeDtypeStruct((segs // 2, total, 2 * rank), jnp.bfloat16)],
        in_specs=[pl.BlockSpec(memory_space=pltpu.SMEM)] + [vmem] * (segs + 1),
        out_specs=[vmem] * (len(group) + 1),
        compiler_params=pltpu.CompilerParams(vmem_limit_bytes=12 << 20),
        cost_estimate=pl.CostEstimate(flops=hint, bytes_accessed=4 * segs * total * width, transcendentals=0),
    )(table, *pieces, down_pool)
    return xs, mine


def project_kernel(x_ref, weight_ref, out_ref):
    out_ref[...] = jnp.dot(x_ref[...], weight_ref[...], preferred_element_type=jnp.float32).astype(jnp.bfloat16)


def project(x, weight, first, count, tile, hint=0):
    width = weight.shape[0]
    rows = x.shape[0]
    return pl.pallas_call(
        project_kernel,
        out_shape=jax.ShapeDtypeStruct((rows, count * tile), jnp.bfloat16),
        grid=(count,),
        in_specs=[
            pl.BlockSpec((rows, width), lambda n: (0, 0)),
            pl.BlockSpec((width, tile), lambda n: (0, first + n)),
        ],
        out_specs=pl.BlockSpec((rows, tile), lambda n: (0, n)),
        compiler_params=pltpu.CompilerParams(vmem_limit_bytes=16 << 20),
        cost_estimate=pl.CostEstimate(
            flops=hint or 2 * rows * width * count * tile, bytes_accessed=2 * width * count * tile, transcendentals=0
        ),
    )(x, pltpu.with_memory_space_constraint(weight, pltpu.HBM))


def low_rank_kernel(first, each, start, widths, tab_ref, inner_ref, *refs):
    parts, ups, out_ref = refs[:2 * len(widths)], refs[2 * len(widths):-1], refs[-1]
    slot = first + pl.program_id(0)
    lanes = inner_ref.shape[2]
    rank = lanes // 2
    rows = out_ref.shape[3]
    lane = lax.broadcasted_iota(jnp.int32, (rows, lanes), 1)
    for e in range(each):
        seg = tab_ref[2, slot * each + e]
        mine = (lane // rank == seg % 2) & (tab_ref[1, slot * each + e] == 1)
        inner = inner_ref[seg // 2][start:start + rows].astype(jnp.float32)
        inner = (jnp.where(mine, inner, 0.0) * low_rank_scale).astype(jnp.bfloat16)
        for which in range(2):
            column = 0
            for n, width in enumerate(widths):
                factor = ups[e][0, which, :, column:column + width]
                low = jnp.dot(inner, jnp.concatenate([factor, factor], axis=0), preferred_element_type=jnp.float32)
                term = parts[which * len(widths) + n][e * rows:(e + 1) * rows].astype(jnp.float32) + low
                out_ref[0, which, e, :, column:column + width] = term.astype(jnp.bfloat16)
                column += width


def add_low_rank(parts, inner, start, rows, first, count, up_pool, table, each, hint=1 << 10):
    columns = up_pool.shape[3]
    rank = up_pool.shape[2]
    widths = [part.shape[1] for part in parts[:len(parts) // 2]]

    def up_spec(e):
        return pl.BlockSpec((1, 2, rank, columns), lambda n, tab: (tab[0, (first + n) * each + e], 0, 0, 0))

    return pl.pallas_call(
        functools.partial(low_rank_kernel, first, each, start, widths),
        out_shape=jax.ShapeDtypeStruct((count, 2, each, rows, columns), jnp.bfloat16),
        grid_spec=pltpu.PrefetchScalarGridSpec(
            num_scalar_prefetch=1,
            grid=(count,),
            in_specs=[pl.BlockSpec(inner.shape, lambda n, tab: (0, 0, 0))]
            + [pl.BlockSpec((each * rows, part.shape[1]), lambda n, tab: (first + n, 0)) for part in parts]
            + [up_spec(e) for e in range(each)],
            out_specs=pl.BlockSpec((1, 2, each, rows, columns), lambda n, tab: (n, 0, 0, 0, 0)),
        ),
        compiler_params=pltpu.CompilerParams(vmem_limit_bytes=24 << 20),
        cost_estimate=pl.CostEstimate(flops=hint, bytes_accessed=1 << 10, transcendentals=0),
    )(table, inner, *parts, *([up_pool] * each))


def add(x, y):
    return (x.astype(jnp.float32) + y.astype(jnp.float32)).astype(x.dtype)


def hop_pairs(level, nseq):
    return [(level, level + 1), (nseq - 1 - level, nseq - 2 - level)]


def scatter_line(own, first, nseq, given=None):
    last = nseq - 2
    arrived = {(0, slot): hop for slot, hop in enumerate(first)}
    arrived.update(given or {})
    for step in range(nseq - 1):
        for level in range(1, step + 1):
            if (level, step) in arrived:
                continue
            slot = step - level if level < nseq // 2 else step
            send = add(own[slot], arrived[level - 1, step - 1])
            arrived[level, step] = lax.ppermute(send, "seq", hop_pairs(level, nseq))
    total = own[nseq - 1].astype(jnp.float32)
    for level in range(nseq - 1):
        total = total + arrived[level, last].astype(jnp.float32)
    return total


def after(x, gate):
    return lax.optimization_barrier((x, gate))[0]


def shards(tokens, gate_weight, up_weight, down_pool, up_pool, req_len, req_adapter, owner_slot):
    nseq = lax.axis_size("seq")
    ntp = lax.axis_size("tp")
    each = ntp // nseq
    me = lax.axis_index("tp")
    place = jnp.arange(ntp, dtype=jnp.int32)
    ordered = chunk_of(place // each, nseq) * each + place % each
    position = jnp.sum(jnp.where(ordered[:, None] == place[None, :], place[:, None], 0), axis=0)
    down_slot, down_here = held(
        slots_of(place, req_len, req_adapter, owner_slot), me * down_pool.shape[0], down_pool.shape[0]
    )
    up_slot, up_here = held(
        slots_of(ordered, req_len, req_adapter, owner_slot),
        lax.axis_index("seq") * up_pool.shape[0],
        up_pool.shape[0],
    )
    down_table = jnp.stack([down_slot, down_here, jnp.full_like(down_slot, me), position])
    up_table = jnp.stack([up_slot, up_here, ordered])
    columns = gate_weight.shape[1]
    tile = 256 if columns % 256 == 0 else 128
    tiles = columns // tile
    (first,), (later,) = GROUPS
    rows = first

    pieces = gather_cores(gather_chips(tokens[:rows], ntp), ntp)
    (x,), mine = assemble(pieces, (first,), down_pool, down_table, 1 << 20)
    x = x.reshape(-1, x.shape[2])
    cuts = [(w, f, c) for w in (gate_weight, up_weight) for f, c in ((0, tiles // 2), (tiles // 2, tiles - tiles // 2))]
    left = list(cuts)

    def piece(gate):
        if not left:
            return None
        weight, begin, count = left.pop(0)
        return project(after(x, gate), weight, begin, count, tile)

    steps, parts = sum_beside(mine.reshape(-1, mine.shape[2]), "tp", ntp, piece)
    shared = steps[-1]
    chips = gather_chips(after(tokens[rows:], steps[-2]), ntp)
    sums, more = sum_beside(shared, "seq", nseq, piece)
    parts = [part for part in parts + more if part is not None]
    inner = sums[-1].reshape(mine.shape)

    def terms(parts, inner, start, rows, first, count, gate, hint=1 << 10):
        given = after(inner, gate) if gate is not None else inner
        return add_low_rank(parts, given, start, rows, first, count, up_pool, up_table, each, hint)

    def first_hop(send):
        return lax.ppermute(send, "seq", hop_pairs(0, nseq))

    head = terms(parts, inner, 0, rows, 0, 1, None)
    pieces = gather_cores(list(after(tuple(chips), head)), ntp)
    (x,), mine = assemble(pieces, (later,), down_pool, down_table, AHEAD)
    head_hop = first_hop(head)
    steps, _ = sum_beside(mine.reshape(-1, mine.shape[2]), "tp", ntp, lambda gate: None)
    shared = steps[-1]
    rest = terms(parts, inner, 0, rows, 1, nseq - 2, shared)
    rest_hop = first_hop(rest)
    kept = terms(parts, inner, 0, rows, nseq - 1, 1, rest)
    inner = sum_one_step(shared, "seq", nseq).reshape(mine.shape)
    second = add(head[0], after(head_hop, rest)[0])
    second_hop = lax.ppermute(second, "seq", hop_pairs(1, nseq))
    x = after(x.reshape(-1, x.shape[2]), (second, kept))
    own = [head[0]] + [rest[slot] for slot in range(nseq - 2)] + [kept[0]]

    rows = later
    parts = [project(x, weight, 0, tiles, tile, AHEAD) for weight in (gate_weight, up_weight)]
    sent = [terms(parts, inner, 0, rows, 0, 1, None)]
    for slot in range(1, nseq):
        sent.append(terms(parts, inner, 0, rows, slot, 1, (sent[-1], second_hop)))
    rest_hop = after(rest_hop, sent[-1])
    third_hop = lax.ppermute(add(rest[0], rest_hop[0]), "seq", hop_pairs(1, nseq))
    hops = []
    for slot in range(nseq - 1):
        hops.append(first_hop(after(sent[slot], hops[slot - 2] if slot > 1 else rest_hop)))

    hops[0] = after(hops[0], third_hop)
    totals = [
        scatter_line(own, [head_hop[0]] + [rest_hop[slot] for slot in range(nseq - 2)], nseq, {(1, 1): second_hop, (1, 2): third_hop}),
        scatter_line([term[0] for term in sent], [hop[0] for hop in hops], nseq),
    ]
    out = [(jax.nn.silu(total[0]) * total[1]).astype(jnp.bfloat16) for total in totals]
    return jnp.concatenate(out, axis=1).reshape(-1, columns)


def solution(mesh):
    placed = (
        P("tp", "seq"),
        P("seq", "tp"),
        P("seq", "tp"),
        P("tp", None, "seq"),
        P("seq", None, None, "tp"),
        P(),
        P(),
        P(),
    )
    return jax.shard_map(
        shards, mesh=mesh, in_specs=placed, out_specs=P("seq", "tp"), check_vma=False
    )
```

```python
import functools

import jax
import jax.numpy as jnp
from jax import lax
from jax.experimental import pallas as pl
from jax.experimental.pallas import tpu as pltpu
from jax.sharding import PartitionSpec as P

SEG_ROWS = 128
GROUPS = ((48,), (80,))
AHEAD = 1 << 36

low_rank_scale = 0.5


def slots_of(segment, req_len, req_adapter, owner_slot):
    order = jnp.arange(req_len.shape[0], dtype=jnp.int32)
    ends = jnp.sum(jnp.where(order[:, None] <= order[None, :], req_len[:, None], 0), axis=0)
    seg_request = jnp.sum((ends[None, :] <= segment[:, None]).astype(jnp.int32), axis=1)
    adapter = jnp.sum(jnp.where(seg_request[:, None] == order[None, :], req_adapter[None, :], 0), axis=1)
    ids = jnp.arange(owner_slot.shape[0], dtype=jnp.int32)
    return jnp.sum(jnp.where(adapter[:, None] == ids[None, :], owner_slot[None, :], 0), axis=1)


def chunk_of(slot, nseq):
    me = lax.axis_index("seq")
    half = me < nseq // 2
    far = jnp.where(half, nseq - 1 - me, me)
    near = slot - far
    far_chunk = jnp.where(half, nseq - 1 - slot, slot)
    near_chunk = jnp.where(half, near, nseq - 1 - near)
    chunk = jnp.where(slot < far, far_chunk, near_chunk)
    return jnp.where(slot == nseq - 1, me, chunk)


def held(seg_slot, first, count):
    local = seg_slot - first
    here = (local >= 0) & (local < count)
    return jnp.clip(local, 0, count - 1), here.astype(jnp.int32)


def swap(x, axis, size, mask):
    return lax.ppermute(x, axis, [(i, i ^ mask) for i in range(size)])


def gather_chips(x, ntp):
    return [x] + [swap(x, "tp", ntp, 2 * m) for m in range(1, ntp // 2)]


def gather_cores(chips, ntp):
    pieces = []
    for piece in chips:
        pieces += [piece, swap(piece, "tp", ntp, 1)]
    return pieces


def sum_one_step(x, axis, size):
    parts = [lax.ppermute(x, axis, [(i, (i + k) % size) for i in range(size)]) for k in range(1, size)]
    total = x.astype(jnp.float32)
    for part in parts:
        total = total + part.astype(jnp.float32)
    return total.astype(x.dtype)


def sum_beside(x, axis, size, beside):
    done = []
    steps = [x]
    mask = 1
    while mask < size:
        other = swap(x, axis, size, mask)
        if mask > 1 or axis != "tp":
            done.append(beside(x))
            other = after(other, done[-1]) if done[-1] is not None else other
        x = add(x, other)
        steps.append(x)
        mask *= 2
    return steps, done


def assemble_kernel(segs, group, tab_ref, *refs):
    pieces, down_ref, xs, inner_ref = refs[:segs], refs[segs], refs[segs + 1:-1], refs[-1]
    me = tab_ref[2, 0]
    for n, piece in enumerate(pieces):
        start = 0
        for x_ref, rows in zip(xs, group):
            x_ref[tab_ref[3, me ^ n]] = piece[start:start + rows]
            start += rows
    start = 0
    for x_ref, rows in zip(xs, group):
        for pair in range(segs // 2):
            halves = []
            for k in (2 * pair, 2 * pair + 1):
                product = lax.dot_general(
                    x_ref[tab_ref[3, k]],
                    down_ref[tab_ref[0, k]],
                    (((1,), (1,)), ((), ())),
                    preferred_element_type=jnp.float32,
                )
                halves.append(product * tab_ref[1, k].astype(jnp.float32))
            inner_ref[pair, start:start + rows] = jnp.concatenate(halves, axis=1).astype(jnp.bfloat16)
        start += rows


def assemble(pieces, group, down_pool, table, hint):
    segs = len(pieces)
    total, width = pieces[0].shape
    rank = down_pool.shape[1]
    vmem = pl.BlockSpec(memory_space=pltpu.VMEM)
    *xs, mine = pl.pallas_call(
        functools.partial(assemble_kernel, segs, group),
        out_shape=[jax.ShapeDtypeStruct((segs, rows, width), jnp.bfloat16) for rows in group]
        + [jax.ShapeDtypeStruct((segs // 2, total, 2 * rank), jnp.bfloat16)],
        in_specs=[pl.BlockSpec(memory_space=pltpu.SMEM)] + [vmem] * (segs + 1),
        out_specs=[vmem] * (len(group) + 1),
        compiler_params=pltpu.CompilerParams(vmem_limit_bytes=12 << 20),
        cost_estimate=pl.CostEstimate(flops=hint, bytes_accessed=4 * segs * total * width, transcendentals=0),
    )(table, *pieces, down_pool)
    return xs, mine


def project_kernel(x_ref, weight_ref, out_ref):
    out_ref[...] = jnp.dot(x_ref[...], weight_ref[...], preferred_element_type=jnp.float32).astype(jnp.bfloat16)


def project(x, weight, first, count, tile, hint=0):
    width = weight.shape[0]
    rows = x.shape[0]
    return pl.pallas_call(
        project_kernel,
        out_shape=jax.ShapeDtypeStruct((rows, count * tile), jnp.bfloat16),
        grid=(count,),
        in_specs=[
            pl.BlockSpec((rows, width), lambda n: (0, 0)),
            pl.BlockSpec((width, tile), lambda n: (0, first + n)),
        ],
        out_specs=pl.BlockSpec((rows, tile), lambda n: (0, n)),
        compiler_params=pltpu.CompilerParams(vmem_limit_bytes=16 << 20),
        cost_estimate=pl.CostEstimate(
            flops=hint or 2 * rows * width * count * tile, bytes_accessed=2 * width * count * tile, transcendentals=0
        ),
    )(x, weight)


def low_rank_kernel(first, each, start, widths, tab_ref, inner_ref, *refs):
    parts, ups, outs = refs[:2 * len(widths)], refs[2 * len(widths):2 * len(widths) + each], refs[2 * len(widths) + each:]
    slot = first + pl.program_id(0)
    lanes = inner_ref.shape[2]
    rank = lanes // 2
    rows = outs[0].shape[3]
    lane = lax.broadcasted_iota(jnp.int32, (rows, lanes), 1)
    for e in range(each):
        seg = tab_ref[2, slot * each + e]
        mine = (lane // rank == seg % 2) & (tab_ref[1, slot * each + e] == 1)
        inner = inner_ref[seg // 2][start:start + rows].astype(jnp.float32)
        inner = (jnp.where(mine, inner, 0.0) * low_rank_scale).astype(jnp.bfloat16)
        for which in range(2):
            column = 0
            for n, width in enumerate(widths):
                factor = ups[e][0, which, :, column:column + width]
                low = jnp.dot(inner, jnp.concatenate([factor, factor], axis=0), preferred_element_type=jnp.float32)
                term = parts[which * len(widths) + n][e * rows:(e + 1) * rows].astype(jnp.float32) + low
                if len(outs) == 2:
                    outs[which][0, 0, e, :, column:column + width] = term.astype(jnp.bfloat16)
                else:
                    outs[0][0, which, e, :, column:column + width] = term.astype(jnp.bfloat16)
                column += width


def add_low_rank(parts, inner, start, rows, first, count, up_pool, table, each, hint=1 << 10, halves=1):
    columns = up_pool.shape[3]
    rank = up_pool.shape[2]
    widths = [part.shape[1] for part in parts[:len(parts) // 2]]

    def up_spec(e):
        return pl.BlockSpec((1, 2, rank, columns), lambda n, tab: (tab[0, (first + n) * each + e], 0, 0, 0))

    return pl.pallas_call(
        functools.partial(low_rank_kernel, first, each, start, widths),
        out_shape=[jax.ShapeDtypeStruct((count, 2 // halves, each, rows, columns), jnp.bfloat16)] * halves,
        grid_spec=pltpu.PrefetchScalarGridSpec(
            num_scalar_prefetch=1,
            grid=(count,),
            in_specs=[pl.BlockSpec(inner.shape, lambda n, tab: (0, 0, 0))]
            + [pl.BlockSpec((each * rows, part.shape[1]), lambda n, tab: (first + n, 0)) for part in parts]
            + [up_spec(e) for e in range(each)],
            out_specs=[pl.BlockSpec((1, 2 // halves, each, rows, columns), lambda n, tab: (n, 0, 0, 0, 0))] * halves,
        ),
        compiler_params=pltpu.CompilerParams(vmem_limit_bytes=24 << 20),
        cost_estimate=pl.CostEstimate(flops=hint, bytes_accessed=1 << 10, transcendentals=0),
    )(table, inner, *parts, *([up_pool] * each))


def add(x, y):
    return (x.astype(jnp.float32) + y.astype(jnp.float32)).astype(x.dtype)


def hop_pairs(level, nseq):
    return [(level, level + 1), (nseq - 1 - level, nseq - 2 - level)]


def scatter_line(own, first, nseq, given=None):
    last = nseq - 2
    arrived = {(0, slot): hop for slot, hop in enumerate(first)}
    arrived.update(given or {})
    for step in range(nseq - 1):
        for level in range(1, step + 1):
            if (level, step) in arrived:
                continue
            slot = step - level if level < nseq // 2 else step
            send = add(own[slot], arrived[level - 1, step - 1])
            arrived[level, step] = lax.ppermute(send, "seq", hop_pairs(level, nseq))
    total = own[nseq - 1].astype(jnp.float32)
    for level in range(nseq - 1):
        total = total + arrived[level, last].astype(jnp.float32)
    return total


def after(x, gate):
    return lax.optimization_barrier((x, gate))[0]


def shards(tokens, gate_weight, up_weight, down_pool, up_pool, req_len, req_adapter, owner_slot):
    nseq = lax.axis_size("seq")
    ntp = lax.axis_size("tp")
    each = ntp // nseq
    me = lax.axis_index("tp")
    place = jnp.arange(ntp, dtype=jnp.int32)
    ordered = chunk_of(place // each, nseq) * each + place % each
    position = jnp.sum(jnp.where(ordered[:, None] == place[None, :], place[:, None], 0), axis=0)
    down_slot, down_here = held(
        slots_of(place, req_len, req_adapter, owner_slot), me * down_pool.shape[0], down_pool.shape[0]
    )
    up_slot, up_here = held(
        slots_of(ordered, req_len, req_adapter, owner_slot),
        lax.axis_index("seq") * up_pool.shape[0],
        up_pool.shape[0],
    )
    down_table = jnp.stack([down_slot, down_here, jnp.full_like(down_slot, me), position])
    up_table = jnp.stack([up_slot, up_here, ordered])
    columns = gate_weight.shape[1]
    tile = 256 if columns % 256 == 0 else 128
    tiles = columns // tile
    (first,), (later,) = GROUPS
    rows = first

    pieces = gather_cores(gather_chips(tokens[:rows], ntp), ntp)
    (x,), mine = assemble(pieces, (first,), down_pool, down_table, 1 << 20)
    x = x.reshape(-1, x.shape[2])
    cuts = [(w, f, c) for w in (gate_weight, up_weight) for f, c in ((0, tiles // 2), (tiles // 2, tiles - tiles // 2))]
    left = list(cuts)

    def piece(gate):
        if not left:
            return None
        weight, begin, count = left.pop(0)
        if weight is gate_weight:
            weight = pltpu.with_memory_space_constraint(weight, pltpu.HBM)
        return project(after(x, gate), weight, begin, count, tile)

    steps, parts = sum_beside(mine.reshape(-1, mine.shape[2]), "tp", ntp, piece)
    shared = steps[-1]
    chips = gather_chips(after(tokens[rows:], steps[-2]), ntp)
    sums, more = sum_beside(shared, "seq", nseq, piece)
    parts = [part for part in parts + more if part is not None]
    inner = sums[-1].reshape(mine.shape)

    def terms(parts, inner, start, rows, first, count, gate, hint=1 << 10, halves=1):
        given = after(inner, gate) if gate is not None else inner
        made = add_low_rank(parts, given, start, rows, first, count, up_pool, up_table, each, hint, halves)
        return made if halves == 2 else made[0]

    def first_hop(send):
        return lax.ppermute(send, "seq", hop_pairs(0, nseq))

    head = terms(parts, inner, 0, rows, 0, 1, None)
    pieces = gather_cores(list(after(tuple(chips), head)), ntp)
    (x,), mine = assemble(pieces, (later,), down_pool, down_table, AHEAD)
    head_hop = first_hop(head)
    steps, _ = sum_beside(mine.reshape(-1, mine.shape[2]), "tp", ntp, lambda gate: None)
    shared = steps[-1]
    rest = terms(parts, inner, 0, rows, 1, nseq - 2, shared)
    rest_hop = first_hop(rest)
    kept = terms(parts, inner, 0, rows, nseq - 1, 1, rest)
    inner = sum_one_step(shared, "seq", nseq).reshape(mine.shape)
    second = add(head[0], after(head_hop, rest)[0])
    second_hop = lax.ppermute(second, "seq", hop_pairs(1, nseq))
    x = after(x.reshape(-1, x.shape[2]), (second, kept))
    own = [head[0]] + [rest[slot] for slot in range(nseq - 2)] + [kept[0]]

    rows = later
    parts = [project(x, weight, 0, tiles, tile, AHEAD) for weight in (gate_weight, up_weight)]
    sent = [terms(parts, inner, 0, rows, 0, 1, None, halves=2)]
    for slot in range(1, nseq):
        sent.append(terms(parts, inner, 0, rows, slot, 1, (sent[-1][0], second_hop), halves=2))
    rest_hop = after(rest_hop, sent[-1][0])
    third_hop = lax.ppermute(add(rest[0], rest_hop[0]), "seq", hop_pairs(1, nseq))
    line = [half for slot in range(nseq - 1) for half in sent[slot]]
    hops = []
    for n, half in enumerate(line):
        hops.append(first_hop(after(half, hops[n - 2] if n > 1 else rest_hop)))
    hops[:2] = after(tuple(hops[:2]), third_hop)

    firsts = [head_hop[0]] + [rest_hop[slot] for slot in range(nseq - 2)]
    totals = [scatter_line(own, firsts, nseq, {(1, 1): second_hop, (1, 2): third_hop})]
    halves = [
        scatter_line([term[which][0, 0] for term in sent], [hop[0, 0] for hop in hops[which::2]], nseq)
        for which in range(2)
    ]
    totals.append(halves)
    out = [(jax.nn.silu(total[0]) * total[1]).astype(jnp.bfloat16) for total in totals]
    return jnp.concatenate(out, axis=1).reshape(-1, columns)


def solution(mesh):
    placed = (
        P("tp", "seq"),
        P("seq", "tp"),
        P("seq", "tp"),
        P("tp", None, "seq"),
        P("seq", None, None, "tp"),
        P(),
        P(),
        P(),
    )
    return jax.shard_map(
        shards, mesh=mesh, in_specs=placed, out_specs=P("seq", "tp"), check_vma=False
    )
```

```python
import functools

import jax
import jax.numpy as jnp
from jax import lax
from jax.experimental import pallas as pl
from jax.experimental.pallas import tpu as pltpu
from jax.sharding import PartitionSpec as P

SEG_ROWS = 128
GROUPS = ((48,), (80,))
AHEAD = 1 << 36

low_rank_scale = 0.5


def slots_of(segment, req_len, req_adapter, owner_slot):
    order = jnp.arange(req_len.shape[0], dtype=jnp.int32)
    ends = jnp.sum(jnp.where(order[:, None] <= order[None, :], req_len[:, None], 0), axis=0)
    seg_request = jnp.sum((ends[None, :] <= segment[:, None]).astype(jnp.int32), axis=1)
    adapter = jnp.sum(jnp.where(seg_request[:, None] == order[None, :], req_adapter[None, :], 0), axis=1)
    ids = jnp.arange(owner_slot.shape[0], dtype=jnp.int32)
    return jnp.sum(jnp.where(adapter[:, None] == ids[None, :], owner_slot[None, :], 0), axis=1)


def chunk_of(slot, nseq):
    me = lax.axis_index("seq")
    half = me < nseq // 2
    far = jnp.where(half, nseq - 1 - me, me)
    near = slot - far
    far_chunk = jnp.where(half, nseq - 1 - slot, slot)
    near_chunk = jnp.where(half, near, nseq - 1 - near)
    chunk = jnp.where(slot < far, far_chunk, near_chunk)
    return jnp.where(slot == nseq - 1, me, chunk)


def held(seg_slot, first, count):
    local = seg_slot - first
    here = (local >= 0) & (local < count)
    return jnp.clip(local, 0, count - 1), here.astype(jnp.int32)


def swap(x, axis, size, mask):
    return lax.ppermute(x, axis, [(i, i ^ mask) for i in range(size)])


def gather_chips(x, ntp):
    return [x] + [swap(x, "tp", ntp, 2 * m) for m in range(1, ntp // 2)]


def gather_cores(chips, ntp):
    pieces = []
    for piece in chips:
        pieces += [piece, swap(piece, "tp", ntp, 1)]
    return pieces


def sum_one_step(x, axis, size):
    parts = [lax.ppermute(x, axis, [(i, (i + k) % size) for i in range(size)]) for k in range(1, size)]
    total = x.astype(jnp.float32)
    for part in parts:
        total = total + part.astype(jnp.float32)
    return total.astype(x.dtype)


def sum_beside(x, axis, size, beside):
    done = []
    steps = [x]
    mask = 1
    while mask < size:
        other = swap(x, axis, size, mask)
        if mask > 1 or axis != "tp":
            done.append(beside(x))
            other = after(other, done[-1]) if done[-1] is not None else other
        x = add(x, other)
        steps.append(x)
        mask *= 2
    return steps, done


def assemble_kernel(segs, group, tab_ref, *refs):
    pieces, down_ref, xs, inner_ref = refs[:segs], refs[segs], refs[segs + 1:-1], refs[-1]
    me = tab_ref[2, 0]
    for n, piece in enumerate(pieces):
        start = 0
        for x_ref, rows in zip(xs, group):
            x_ref[tab_ref[3, me ^ n]] = piece[start:start + rows]
            start += rows
    start = 0
    for x_ref, rows in zip(xs, group):
        for pair in range(segs // 2):
            halves = []
            for k in (2 * pair, 2 * pair + 1):
                product = lax.dot_general(
                    x_ref[tab_ref[3, k]],
                    down_ref[tab_ref[0, k]],
                    (((1,), (1,)), ((), ())),
                    preferred_element_type=jnp.float32,
                )
                halves.append(product * tab_ref[1, k].astype(jnp.float32))
            inner_ref[pair, start:start + rows] = jnp.concatenate(halves, axis=1).astype(jnp.bfloat16)
        start += rows


def assemble(pieces, group, down_pool, table, hint):
    segs = len(pieces)
    total, width = pieces[0].shape
    rank = down_pool.shape[1]
    vmem = pl.BlockSpec(memory_space=pltpu.VMEM)
    *xs, mine = pl.pallas_call(
        functools.partial(assemble_kernel, segs, group),
        out_shape=[jax.ShapeDtypeStruct((segs, rows, width), jnp.bfloat16) for rows in group]
        + [jax.ShapeDtypeStruct((segs // 2, total, 2 * rank), jnp.bfloat16)],
        in_specs=[pl.BlockSpec(memory_space=pltpu.SMEM)] + [vmem] * (segs + 1),
        out_specs=[vmem] * (len(group) + 1),
        compiler_params=pltpu.CompilerParams(vmem_limit_bytes=12 << 20),
        cost_estimate=pl.CostEstimate(flops=hint, bytes_accessed=4 * segs * total * width, transcendentals=0),
    )(table, *pieces, down_pool)
    return xs, mine


def project_kernel(x_ref, weight_ref, out_ref):
    out_ref[...] = jnp.dot(x_ref[...], weight_ref[...], preferred_element_type=jnp.float32).astype(jnp.bfloat16)


def project(x, weight, first, count, tile, hint=0):
    width = weight.shape[0]
    rows = x.shape[0]
    return pl.pallas_call(
        project_kernel,
        out_shape=jax.ShapeDtypeStruct((rows, count * tile), jnp.bfloat16),
        grid=(count,),
        in_specs=[
            pl.BlockSpec((rows, width), lambda n: (0, 0)),
            pl.BlockSpec((width, tile), lambda n: (0, first + n)),
        ],
        out_specs=pl.BlockSpec((rows, tile), lambda n: (0, n)),
        compiler_params=pltpu.CompilerParams(vmem_limit_bytes=16 << 20),
        cost_estimate=pl.CostEstimate(
            flops=hint or 2 * rows * width * count * tile, bytes_accessed=2 * width * count * tile, transcendentals=0
        ),
    )(x, weight)


def low_rank_kernel(first, each, start, widths, tab_ref, inner_ref, *refs):
    parts, ups, out_ref = refs[:2 * len(widths)], refs[2 * len(widths):-1], refs[-1]
    slot = first + pl.program_id(0)
    lanes = inner_ref.shape[2]
    rank = lanes // 2
    rows = out_ref.shape[3]
    lane = lax.broadcasted_iota(jnp.int32, (rows, lanes), 1)
    for e in range(each):
        seg = tab_ref[2, slot * each + e]
        mine = (lane // rank == seg % 2) & (tab_ref[1, slot * each + e] == 1)
        inner = inner_ref[seg // 2][start:start + rows].astype(jnp.float32)
        inner = (jnp.where(mine, inner, 0.0) * low_rank_scale).astype(jnp.bfloat16)
        for which in range(2):
            column = 0
            for n, width in enumerate(widths):
                factor = ups[e][0, which, :, column:column + width]
                low = jnp.dot(inner, jnp.concatenate([factor, factor], axis=0), preferred_element_type=jnp.float32)
                term = parts[which * len(widths) + n][e * rows:(e + 1) * rows].astype(jnp.float32) + low
                out_ref[0, which, e, :, column:column + width] = term.astype(jnp.bfloat16)
                column += width


def add_low_rank(parts, inner, start, rows, first, count, up_pool, table, each, hint=1 << 10):
    columns = up_pool.shape[3]
    rank = up_pool.shape[2]
    widths = [part.shape[1] for part in parts[:len(parts) // 2]]

    def up_spec(e):
        return pl.BlockSpec((1, 2, rank, columns), lambda n, tab: (tab[0, (first + n) * each + e], 0, 0, 0))

    return pl.pallas_call(
        functools.partial(low_rank_kernel, first, each, start, widths),
        out_shape=jax.ShapeDtypeStruct((count, 2, each, rows, columns), jnp.bfloat16),
        grid_spec=pltpu.PrefetchScalarGridSpec(
            num_scalar_prefetch=1,
            grid=(count,),
            in_specs=[pl.BlockSpec(inner.shape, lambda n, tab: (0, 0, 0))]
            + [pl.BlockSpec((each * rows, part.shape[1]), lambda n, tab: (first + n, 0)) for part in parts]
            + [up_spec(e) for e in range(each)],
            out_specs=pl.BlockSpec((1, 2, each, rows, columns), lambda n, tab: (n, 0, 0, 0, 0)),
        ),
        compiler_params=pltpu.CompilerParams(vmem_limit_bytes=24 << 20),
        cost_estimate=pl.CostEstimate(flops=hint, bytes_accessed=1 << 10, transcendentals=0),
    )(table, inner, *parts, *([up_pool] * each))


def add(x, y):
    return (x.astype(jnp.float32) + y.astype(jnp.float32)).astype(x.dtype)


def hop_pairs(level, nseq):
    return [(level, level + 1), (nseq - 1 - level, nseq - 2 - level)]


def scatter_line(own, first, nseq, given=None):
    last = nseq - 2
    arrived = {(0, slot): hop for slot, hop in enumerate(first)}
    arrived.update(given or {})
    for step in range(nseq - 1):
        for level in range(1, step + 1):
            if (level, step) in arrived:
                continue
            slot = step - level if level < nseq // 2 else step
            send = add(own[slot], arrived[level - 1, step - 1])
            arrived[level, step] = lax.ppermute(send, "seq", hop_pairs(level, nseq))
    total = own[nseq - 1].astype(jnp.float32)
    for level in range(nseq - 1):
        total = total + arrived[level, last].astype(jnp.float32)
    return total


def after(x, gate):
    return lax.optimization_barrier((x, gate))[0]


def shards(tokens, gate_weight, up_weight, down_pool, up_pool, req_len, req_adapter, owner_slot):
    nseq = lax.axis_size("seq")
    ntp = lax.axis_size("tp")
    each = ntp // nseq
    me = lax.axis_index("tp")
    place = jnp.arange(ntp, dtype=jnp.int32)
    ordered = chunk_of(place // each, nseq) * each + place % each
    position = jnp.sum(jnp.where(ordered[:, None] == place[None, :], place[:, None], 0), axis=0)
    down_slot, down_here = held(
        slots_of(place, req_len, req_adapter, owner_slot), me * down_pool.shape[0], down_pool.shape[0]
    )
    up_slot, up_here = held(
        slots_of(ordered, req_len, req_adapter, owner_slot),
        lax.axis_index("seq") * up_pool.shape[0],
        up_pool.shape[0],
    )
    down_table = jnp.stack([down_slot, down_here, jnp.full_like(down_slot, me), position])
    up_table = jnp.stack([up_slot, up_here, ordered])
    columns = gate_weight.shape[1]
    tile = 256 if columns % 256 == 0 else 128
    tiles = columns // tile
    (first,), (later,) = GROUPS
    rows = first

    pieces = gather_cores(gather_chips(tokens[:rows], ntp), ntp)
    (x,), mine = assemble(pieces, (first,), down_pool, down_table, 1 << 20)
    x = x.reshape(-1, x.shape[2])
    cuts = [(w, f, c) for w in (gate_weight, up_weight) for f, c in ((0, tiles // 2), (tiles // 2, tiles - tiles // 2))]
    left = list(cuts)

    def piece(gate):
        if not left:
            return None
        weight, begin, count = left.pop(0)
        if weight is gate_weight:
            weight = pltpu.with_memory_space_constraint(weight, pltpu.HBM)
        return project(after(x, gate), weight, begin, count, tile)

    steps, parts = sum_beside(mine.reshape(-1, mine.shape[2]), "tp", ntp, piece)
    shared = steps[-1]
    chips = gather_chips(after(tokens[rows:], steps[-2]), ntp)
    sums, more = sum_beside(shared, "seq", nseq, piece)
    parts = [part for part in parts + more if part is not None]
    inner = sums[-1].reshape(mine.shape)

    def terms(parts, inner, start, rows, first, count, gate, hint=1 << 10):
        given = after(inner, gate) if gate is not None else inner
        return add_low_rank(parts, given, start, rows, first, count, up_pool, up_table, each, hint)

    def first_hop(send):
        return lax.ppermute(send, "seq", hop_pairs(0, nseq))

    head = terms(parts, inner, 0, rows, 0, 1, None)
    pieces = gather_cores(list(after(tuple(chips), head)), ntp)
    (x,), mine = assemble(pieces, (later,), down_pool, down_table, AHEAD)
    head_hop = first_hop(head)
    steps, _ = sum_beside(mine.reshape(-1, mine.shape[2]), "tp", ntp, lambda gate: None)
    shared = steps[-1]
    rest = terms(parts, inner, 0, rows, 1, nseq - 2, shared)
    rest_hop = first_hop(rest)
    kept = terms(parts, inner, 0, rows, nseq - 1, 1, rest)
    inner = sum_one_step(shared, "seq", nseq).reshape(mine.shape)
    second = add(head[0], after(head_hop, rest)[0])
    second_hop = lax.ppermute(second, "seq", hop_pairs(1, nseq))
    x = after(x.reshape(-1, x.shape[2]), (second, kept))
    own = [head[0]] + [rest[slot] for slot in range(nseq - 2)] + [kept[0]]

    rows = later
    parts = [project(x, weight, 0, tiles, tile, AHEAD) for weight in (gate_weight, up_weight)]
    sent = [terms(parts, inner, 0, rows, 0, 1, None)]
    for slot in range(1, nseq):
        sent.append(terms(parts, inner, 0, rows, slot, 1, (sent[-1], second_hop)))
    rest_hop = after(rest_hop, sent[-1])
    third_hop = lax.ppermute(add(rest[0], rest_hop[0]), "seq", hop_pairs(1, nseq))
    hops = []
    for slot in range(nseq - 1):
        hops.append(first_hop(after(sent[slot], hops[slot - 2] if slot > 1 else rest_hop)))

    hops[0] = after(hops[0], third_hop)
    totals = [
        scatter_line(own, [head_hop[0]] + [rest_hop[slot] for slot in range(nseq - 2)], nseq, {(1, 1): second_hop, (1, 2): third_hop}),
        scatter_line([term[0] for term in sent], [hop[0] for hop in hops], nseq),
    ]
    out = [(jax.nn.silu(total[0]) * total[1]).astype(jnp.bfloat16) for total in totals]
    return jnp.concatenate(out, axis=1).reshape(-1, columns)


def solution(mesh):
    placed = (
        P("tp", "seq"),
        P("seq", "tp"),
        P("seq", "tp"),
        P("tp", None, "seq"),
        P("seq", None, None, "tp"),
        P(),
        P(),
        P(),
    )
    return jax.shard_map(
        shards, mesh=mesh, in_specs=placed, out_specs=P("seq", "tp"), check_vma=False
    )
```

```python
import functools

import jax
import jax.numpy as jnp
from jax import lax
from jax.experimental import pallas as pl
from jax.experimental.pallas import tpu as pltpu
from jax.sharding import PartitionSpec as P

SEG_ROWS = 128
GROUPS = ((48,), (80,))
AHEAD = 1 << 36

low_rank_scale = 0.5


def slots_of(segment, req_len, req_adapter, owner_slot):
    order = jnp.arange(req_len.shape[0], dtype=jnp.int32)
    ends = jnp.sum(jnp.where(order[:, None] <= order[None, :], req_len[:, None], 0), axis=0)
    seg_request = jnp.sum((ends[None, :] <= segment[:, None]).astype(jnp.int32), axis=1)
    adapter = jnp.sum(jnp.where(seg_request[:, None] == order[None, :], req_adapter[None, :], 0), axis=1)
    ids = jnp.arange(owner_slot.shape[0], dtype=jnp.int32)
    return jnp.sum(jnp.where(adapter[:, None] == ids[None, :], owner_slot[None, :], 0), axis=1)


def chunk_of(slot, nseq):
    me = lax.axis_index("seq")
    half = me < nseq // 2
    far = jnp.where(half, nseq - 1 - me, me)
    near = slot - far
    far_chunk = jnp.where(half, nseq - 1 - slot, slot)
    near_chunk = jnp.where(half, near, nseq - 1 - near)
    chunk = jnp.where(slot < far, far_chunk, near_chunk)
    return jnp.where(slot == nseq - 1, me, chunk)


def held(seg_slot, first, count):
    local = seg_slot - first
    here = (local >= 0) & (local < count)
    return jnp.clip(local, 0, count - 1), here.astype(jnp.int32)


def swap(x, axis, size, mask):
    return lax.ppermute(x, axis, [(i, i ^ mask) for i in range(size)])


def gather_chips(x, ntp):
    return [x] + [swap(x, "tp", ntp, 2 * m) for m in range(1, ntp // 2)]


def gather_cores(chips, ntp):
    pieces = []
    for piece in chips:
        pieces += [piece, swap(piece, "tp", ntp, 1)]
    return pieces


def sum_one_step(x, axis, size):
    parts = [lax.ppermute(x, axis, [(i, (i + k) % size) for i in range(size)]) for k in range(1, size)]
    total = x.astype(jnp.float32)
    for part in parts:
        total = total + part.astype(jnp.float32)
    return total.astype(x.dtype)


def sum_beside(x, axis, size, beside):
    done = []
    steps = [x]
    mask = 1
    while mask < size:
        other = swap(x, axis, size, mask)
        if mask > 1 or axis != "tp":
            done.append(beside(x))
            other = after(other, done[-1]) if done[-1] is not None else other
        x = add(x, other)
        steps.append(x)
        mask *= 2
    return steps, done


def assemble_kernel(segs, group, tab_ref, *refs):
    pieces, down_ref, xs, inner_ref = refs[:segs], refs[segs], refs[segs + 1:-1], refs[-1]
    me = tab_ref[2, 0]
    for n, piece in enumerate(pieces):
        start = 0
        for x_ref, rows in zip(xs, group):
            x_ref[tab_ref[3, me ^ n]] = piece[start:start + rows]
            start += rows
    start = 0
    for x_ref, rows in zip(xs, group):
        for pair in range(segs // 2):
            halves = []
            for k in (2 * pair, 2 * pair + 1):
                product = lax.dot_general(
                    x_ref[tab_ref[3, k]],
                    down_ref[tab_ref[0, k]],
                    (((1,), (1,)), ((), ())),
                    preferred_element_type=jnp.float32,
                )
                halves.append(product * tab_ref[1, k].astype(jnp.float32))
            inner_ref[pair, start:start + rows] = jnp.concatenate(halves, axis=1).astype(jnp.bfloat16)
        start += rows


def assemble(pieces, group, down_pool, table, hint):
    segs = len(pieces)
    total, width = pieces[0].shape
    rank = down_pool.shape[1]
    vmem = pl.BlockSpec(memory_space=pltpu.VMEM)
    *xs, mine = pl.pallas_call(
        functools.partial(assemble_kernel, segs, group),
        out_shape=[jax.ShapeDtypeStruct((segs, rows, width), jnp.bfloat16) for rows in group]
        + [jax.ShapeDtypeStruct((segs // 2, total, 2 * rank), jnp.bfloat16)],
        in_specs=[pl.BlockSpec(memory_space=pltpu.SMEM)] + [vmem] * (segs + 1),
        out_specs=[vmem] * (len(group) + 1),
        compiler_params=pltpu.CompilerParams(vmem_limit_bytes=12 << 20),
        cost_estimate=pl.CostEstimate(flops=hint, bytes_accessed=4 * segs * total * width, transcendentals=0),
    )(table, *pieces, down_pool)
    return xs, mine


def project_kernel(x_ref, weight_ref, out_ref):
    out_ref[...] = jnp.dot(x_ref[...], weight_ref[...], preferred_element_type=jnp.float32).astype(jnp.bfloat16)


def project(x, weight, first, count, tile, hint=0):
    width = weight.shape[0]
    rows = x.shape[0]
    return pl.pallas_call(
        project_kernel,
        out_shape=jax.ShapeDtypeStruct((rows, count * tile), jnp.bfloat16),
        grid=(count,),
        in_specs=[
            pl.BlockSpec((rows, width), lambda n: (0, 0)),
            pl.BlockSpec((width, tile), lambda n: (0, first + n)),
        ],
        out_specs=pl.BlockSpec((rows, tile), lambda n: (0, n)),
        compiler_params=pltpu.CompilerParams(vmem_limit_bytes=16 << 20),
        cost_estimate=pl.CostEstimate(
            flops=hint or 2 * rows * width * count * tile, bytes_accessed=2 * width * count * tile, transcendentals=0
        ),
    )(x, weight)


def low_rank_kernel(first, each, start, widths, tab_ref, inner_ref, *refs):
    parts, ups, out_ref = refs[:2 * len(widths)], refs[2 * len(widths):-1], refs[-1]
    slot = first + pl.program_id(0)
    lanes = inner_ref.shape[2]
    rank = lanes // 2
    rows = out_ref.shape[3]
    lane = lax.broadcasted_iota(jnp.int32, (rows, lanes), 1)
    for e in range(each):
        seg = tab_ref[2, slot * each + e]
        mine = (lane // rank == seg % 2) & (tab_ref[1, slot * each + e] == 1)
        inner = inner_ref[seg // 2][start:start + rows].astype(jnp.float32)
        inner = (jnp.where(mine, inner, 0.0) * low_rank_scale).astype(jnp.bfloat16)
        for which in range(2):
            column = 0
            for n, width in enumerate(widths):
                factor = ups[e][0, which, :, column:column + width]
                low = jnp.dot(inner, jnp.concatenate([factor, factor], axis=0), preferred_element_type=jnp.float32)
                term = parts[which * len(widths) + n][e * rows:(e + 1) * rows].astype(jnp.float32) + low
                out_ref[0, which, e, :, column:column + width] = term.astype(jnp.bfloat16)
                column += width


def add_low_rank(parts, inner, start, rows, first, count, up_pool, table, each, hint=1 << 10):
    columns = up_pool.shape[3]
    rank = up_pool.shape[2]
    widths = [part.shape[1] for part in parts[:len(parts) // 2]]

    def up_spec(e):
        return pl.BlockSpec((1, 2, rank, columns), lambda n, tab: (tab[0, (first + n) * each + e], 0, 0, 0))

    return pl.pallas_call(
        functools.partial(low_rank_kernel, first, each, start, widths),
        out_shape=jax.ShapeDtypeStruct((count, 2, each, rows, columns), jnp.bfloat16),
        grid_spec=pltpu.PrefetchScalarGridSpec(
            num_scalar_prefetch=1,
            grid=(count,),
            in_specs=[pl.BlockSpec(inner.shape, lambda n, tab: (0, 0, 0))]
            + [pl.BlockSpec((each * rows, part.shape[1]), lambda n, tab: (first + n, 0)) for part in parts]
            + [up_spec(e) for e in range(each)],
            out_specs=pl.BlockSpec((1, 2, each, rows, columns), lambda n, tab: (n, 0, 0, 0, 0)),
        ),
        compiler_params=pltpu.CompilerParams(vmem_limit_bytes=24 << 20),
        cost_estimate=pl.CostEstimate(flops=hint, bytes_accessed=1 << 10, transcendentals=0),
    )(table, inner, *parts, *([up_pool] * each))


def add(x, y):
    return (x.astype(jnp.float32) + y.astype(jnp.float32)).astype(x.dtype)


def hop_pairs(level, nseq):
    return [(level, level + 1), (nseq - 1 - level, nseq - 2 - level)]


def scatter_line(own, first, nseq, given=None):
    last = nseq - 2
    arrived = {(0, slot): hop for slot, hop in enumerate(first)}
    arrived.update(given or {})
    for step in range(nseq - 1):
        for level in range(1, step + 1):
            if (level, step) in arrived:
                continue
            slot = step - level if level < nseq // 2 else step
            send = add(own[slot], arrived[level - 1, step - 1])
            arrived[level, step] = lax.ppermute(send, "seq", hop_pairs(level, nseq))
    totals = []
    for which in range(2):
        total = own[nseq - 1][which].astype(jnp.float32)
        for level in range(nseq - 1):
            total = total + arrived[level, last][which].astype(jnp.float32)
        totals.append(total)
    return totals


def after(x, gate):
    return lax.optimization_barrier((x, gate))[0]


def shards(tokens, gate_weight, up_weight, down_pool, up_pool, req_len, req_adapter, owner_slot):
    nseq = lax.axis_size("seq")
    ntp = lax.axis_size("tp")
    each = ntp // nseq
    me = lax.axis_index("tp")
    place = jnp.arange(ntp, dtype=jnp.int32)
    ordered = chunk_of(place // each, nseq) * each + place % each
    position = jnp.sum(jnp.where(ordered[:, None] == place[None, :], place[:, None], 0), axis=0)
    down_slot, down_here = held(
        slots_of(place, req_len, req_adapter, owner_slot), me * down_pool.shape[0], down_pool.shape[0]
    )
    up_slot, up_here = held(
        slots_of(ordered, req_len, req_adapter, owner_slot),
        lax.axis_index("seq") * up_pool.shape[0],
        up_pool.shape[0],
    )
    down_table = jnp.stack([down_slot, down_here, jnp.full_like(down_slot, me), position])
    up_table = jnp.stack([up_slot, up_here, ordered])
    columns = gate_weight.shape[1]
    tile = 256 if columns % 256 == 0 else 128
    tiles = columns // tile
    (first,), (later,) = GROUPS
    rows = first

    pieces = gather_cores(gather_chips(tokens[:rows], ntp), ntp)
    (x,), mine = assemble(pieces, (first,), down_pool, down_table, 1 << 20)
    x = x.reshape(-1, x.shape[2])
    cuts = [(w, f, c) for w in (gate_weight, up_weight) for f, c in ((0, tiles // 2), (tiles // 2, tiles - tiles // 2))]
    left = list(cuts)

    def piece(gate):
        if not left:
            return None
        weight, begin, count = left.pop(0)
        if weight is gate_weight:
            weight = pltpu.with_memory_space_constraint(weight, pltpu.HBM)
        return project(after(x, gate), weight, begin, count, tile)

    steps, parts = sum_beside(mine.reshape(-1, mine.shape[2]), "tp", ntp, piece)
    shared = steps[-1]
    chips = gather_chips(after(tokens[rows:], steps[-2]), ntp)
    sums, more = sum_beside(shared, "seq", nseq, piece)
    parts = [part for part in parts + more if part is not None]
    inner = sums[-1].reshape(mine.shape)

    def terms(parts, inner, start, rows, first, count, gate, hint=1 << 10):
        given = after(inner, gate) if gate is not None else inner
        return add_low_rank(parts, given, start, rows, first, count, up_pool, up_table, each, hint)

    def first_hop(send):
        return lax.ppermute(send, "seq", hop_pairs(0, nseq))

    head = terms(parts, inner, 0, rows, 0, 1, None)
    pieces = gather_cores(list(after(tuple(chips), head)), ntp)
    (x,), mine = assemble(pieces, (later,), down_pool, down_table, AHEAD)
    head_hop = first_hop(head)
    steps, _ = sum_beside(mine.reshape(-1, mine.shape[2]), "tp", ntp, lambda gate: None)
    shared = steps[-1]
    rest = terms(parts, inner, 0, rows, 1, nseq - 2, mine)
    kept = terms(parts, inner, 0, rows, nseq - 1, 1, (rest, shared))
    rest_hop = first_hop(after(rest, kept))
    inner = sum_one_step(shared, "seq", nseq).reshape(mine.shape)
    second = add(head[0], after(head_hop, rest)[0])
    second_hop = lax.ppermute(second, "seq", hop_pairs(1, nseq))
    x = after(x.reshape(-1, x.shape[2]), (second, kept))
    own = [head[0]] + [rest[slot] for slot in range(nseq - 2)] + [kept[0]]

    rows = later
    gate_part = project(x, gate_weight, 0, tiles, tile, AHEAD)
    parts = [gate_part, project(after(x, gate_part), up_weight, 0, tiles, tile, 1 << 10)]
    sent = [terms(parts, inner, 0, rows, 0, 1, None)]
    for slot in range(1, nseq):
        sent.append(terms(parts, inner, 0, rows, slot, 1, (sent[-1], second_hop)))
    rest_hop = after(rest_hop, sent[-1])
    third_hop = lax.ppermute(add(rest[0], rest_hop[0]), "seq", hop_pairs(1, nseq))
    hops = []
    for slot in range(nseq - 1):
        hops.append(first_hop(after(sent[slot], hops[slot - 2] if slot > 1 else rest_hop)))

    hops[0] = after(hops[0], third_hop)
    totals = [
        scatter_line(own, [head_hop[0]] + [rest_hop[slot] for slot in range(nseq - 2)], nseq, {(1, 1): second_hop, (1, 2): third_hop}),
        scatter_line([term[0] for term in sent], [hop[0] for hop in hops], nseq),
    ]
    out = [(jax.nn.silu(total[0]) * total[1]).astype(jnp.bfloat16) for total in totals]
    return jnp.concatenate(out, axis=1).reshape(-1, columns)


def solution(mesh):
    placed = (
        P("tp", "seq"),
        P("seq", "tp"),
        P("seq", "tp"),
        P("tp", None, "seq"),
        P("seq", None, None, "tp"),
        P(),
        P(),
        P(),
    )
    return jax.shard_map(
        shards, mesh=mesh, in_specs=placed, out_specs=P("seq", "tp"), check_vma=False
    )
```

```python
import functools

import jax
import jax.numpy as jnp
from jax import lax
from jax.experimental import pallas as pl
from jax.experimental.pallas import tpu as pltpu
from jax.sharding import PartitionSpec as P

SEG_ROWS = 128
GROUPS = ((48,), (80,))
AHEAD = 1 << 36

low_rank_scale = 0.5


def slots_of(segment, req_len, req_adapter, owner_slot):
    order = jnp.arange(req_len.shape[0], dtype=jnp.int32)
    ends = jnp.sum(jnp.where(order[:, None] <= order[None, :], req_len[:, None], 0), axis=0)
    seg_request = jnp.sum((ends[None, :] <= segment[:, None]).astype(jnp.int32), axis=1)
    adapter = jnp.sum(jnp.where(seg_request[:, None] == order[None, :], req_adapter[None, :], 0), axis=1)
    ids = jnp.arange(owner_slot.shape[0], dtype=jnp.int32)
    return jnp.sum(jnp.where(adapter[:, None] == ids[None, :], owner_slot[None, :], 0), axis=1)


def chunk_of(slot, nseq):
    me = lax.axis_index("seq")
    half = me < nseq // 2
    far = jnp.where(half, nseq - 1 - me, me)
    near = slot - far
    far_chunk = jnp.where(half, nseq - 1 - slot, slot)
    near_chunk = jnp.where(half, near, nseq - 1 - near)
    chunk = jnp.where(slot < far, far_chunk, near_chunk)
    return jnp.where(slot == nseq - 1, me, chunk)


def held(seg_slot, first, count):
    local = seg_slot - first
    here = (local >= 0) & (local < count)
    return jnp.clip(local, 0, count - 1), here.astype(jnp.int32)


def swap(x, axis, size, mask):
    return lax.ppermute(x, axis, [(i, i ^ mask) for i in range(size)])


def gather_chips(x, ntp):
    return [x] + [swap(x, "tp", ntp, 2 * m) for m in range(1, ntp // 2)]


def gather_cores(chips, ntp):
    pieces = []
    for piece in chips:
        pieces += [piece, swap(piece, "tp", ntp, 1)]
    return pieces


def sum_one_step(x, axis, size):
    parts = [lax.ppermute(x, axis, [(i, (i + k) % size) for i in range(size)]) for k in range(1, size)]
    total = x.astype(jnp.float32)
    for part in parts:
        total = total + part.astype(jnp.float32)
    return total.astype(x.dtype)


def sum_beside(x, axis, size, beside):
    done = []
    steps = [x]
    mask = 1
    while mask < size:
        other = swap(x, axis, size, mask)
        if mask > 1 or axis != "tp":
            done.append(beside(x))
            other = after(other, done[-1]) if done[-1] is not None else other
        x = add(x, other)
        steps.append(x)
        mask *= 2
    return steps, done


def assemble_kernel(segs, group, tab_ref, *refs):
    pieces, down_ref, xs, inner_ref = refs[:segs], refs[segs], refs[segs + 1:-1], refs[-1]
    me = tab_ref[2, 0]
    for n, piece in enumerate(pieces):
        start = 0
        for x_ref, rows in zip(xs, group):
            x_ref[tab_ref[3, me ^ n]] = piece[start:start + rows]
            start += rows
    start = 0
    for x_ref, rows in zip(xs, group):
        for pair in range(segs // 2):
            halves = []
            for k in (2 * pair, 2 * pair + 1):
                product = lax.dot_general(
                    x_ref[tab_ref[3, k]],
                    down_ref[tab_ref[0, k]],
                    (((1,), (1,)), ((), ())),
                    preferred_element_type=jnp.float32,
                )
                halves.append(product * tab_ref[1, k].astype(jnp.float32))
            inner_ref[pair, start:start + rows] = jnp.concatenate(halves, axis=1).astype(jnp.bfloat16)
        start += rows


def assemble(pieces, group, down_pool, table, hint):
    segs = len(pieces)
    total, width = pieces[0].shape
    rank = down_pool.shape[1]
    vmem = pl.BlockSpec(memory_space=pltpu.VMEM)
    *xs, mine = pl.pallas_call(
        functools.partial(assemble_kernel, segs, group),
        out_shape=[jax.ShapeDtypeStruct((segs, rows, width), jnp.bfloat16) for rows in group]
        + [jax.ShapeDtypeStruct((segs // 2, total, 2 * rank), jnp.bfloat16)],
        in_specs=[pl.BlockSpec(memory_space=pltpu.SMEM)] + [vmem] * (segs + 1),
        out_specs=[vmem] * (len(group) + 1),
        compiler_params=pltpu.CompilerParams(vmem_limit_bytes=12 << 20),
        cost_estimate=pl.CostEstimate(flops=hint, bytes_accessed=4 * segs * total * width, transcendentals=0),
    )(table, *pieces, down_pool)
    return xs, mine


def project_kernel(x_ref, weight_ref, out_ref):
    out_ref[...] = jnp.dot(x_ref[...], weight_ref[...], preferred_element_type=jnp.float32).astype(jnp.bfloat16)


def project(x, weight, first, count, tile, hint=0):
    width = weight.shape[0]
    rows = x.shape[0]
    return pl.pallas_call(
        project_kernel,
        out_shape=jax.ShapeDtypeStruct((rows, count * tile), jnp.bfloat16),
        grid=(count,),
        in_specs=[
            pl.BlockSpec((rows, width), lambda n: (0, 0)),
            pl.BlockSpec((width, tile), lambda n: (0, first + n)),
        ],
        out_specs=pl.BlockSpec((rows, tile), lambda n: (0, n)),
        compiler_params=pltpu.CompilerParams(vmem_limit_bytes=16 << 20),
        cost_estimate=pl.CostEstimate(
            flops=hint or 2 * rows * width * count * tile, bytes_accessed=2 * width * count * tile, transcendentals=0
        ),
    )(x, weight)


def low_rank_kernel(first, each, start, widths, tab_ref, inner_ref, *refs):
    parts, ups, out_ref = refs[:2 * len(widths)], refs[2 * len(widths):-1], refs[-1]
    slot = first + pl.program_id(0)
    lanes = inner_ref.shape[2]
    rank = lanes // 2
    rows = out_ref.shape[3]
    lane = lax.broadcasted_iota(jnp.int32, (rows, lanes), 1)
    for e in range(each):
        seg = tab_ref[2, slot * each + e]
        mine = (lane // rank == seg % 2) & (tab_ref[1, slot * each + e] == 1)
        inner = inner_ref[seg // 2][start:start + rows].astype(jnp.float32)
        inner = (jnp.where(mine, inner, 0.0) * low_rank_scale).astype(jnp.bfloat16)
        for which in range(2):
            column = 0
            for n, width in enumerate(widths):
                factor = ups[e][0, which, :, column:column + width]
                low = jnp.dot(inner, jnp.concatenate([factor, factor], axis=0), preferred_element_type=jnp.float32)
                term = parts[which * len(widths) + n][e * rows:(e + 1) * rows].astype(jnp.float32) + low
                out_ref[0, which, e, :, column:column + width] = term.astype(jnp.bfloat16)
                column += width


def add_low_rank(parts, inner, start, rows, first, count, up_pool, table, each, hint=1 << 10):
    columns = up_pool.shape[3]
    rank = up_pool.shape[2]
    widths = [part.shape[1] for part in parts[:len(parts) // 2]]

    def up_spec(e):
        return pl.BlockSpec((1, 2, rank, columns), lambda n, tab: (tab[0, (first + n) * each + e], 0, 0, 0))

    return pl.pallas_call(
        functools.partial(low_rank_kernel, first, each, start, widths),
        out_shape=jax.ShapeDtypeStruct((count, 2, each, rows, columns), jnp.bfloat16),
        grid_spec=pltpu.PrefetchScalarGridSpec(
            num_scalar_prefetch=1,
            grid=(count,),
            in_specs=[pl.BlockSpec(inner.shape, lambda n, tab: (0, 0, 0))]
            + [pl.BlockSpec((each * rows, part.shape[1]), lambda n, tab: (first + n, 0)) for part in parts]
            + [up_spec(e) for e in range(each)],
            out_specs=pl.BlockSpec((1, 2, each, rows, columns), lambda n, tab: (n, 0, 0, 0, 0)),
        ),
        compiler_params=pltpu.CompilerParams(vmem_limit_bytes=24 << 20),
        cost_estimate=pl.CostEstimate(flops=hint, bytes_accessed=1 << 10, transcendentals=0),
    )(table, inner, *parts, *([up_pool] * each))


def add(x, y):
    return (x.astype(jnp.float32) + y.astype(jnp.float32)).astype(x.dtype)


def hop_pairs(level, nseq):
    return [(level, level + 1), (nseq - 1 - level, nseq - 2 - level)]


def scatter_line(own, first, nseq, given=None):
    last = nseq - 2
    arrived = {(0, slot): hop for slot, hop in enumerate(first)}
    arrived.update(given or {})
    for step in range(nseq - 1):
        for level in range(1, step + 1):
            if (level, step) in arrived:
                continue
            slot = step - level if level < nseq // 2 else step
            send = add(own[slot], arrived[level - 1, step - 1])
            arrived[level, step] = lax.ppermute(send, "seq", hop_pairs(level, nseq))
    totals = []
    for which in range(2):
        total = own[nseq - 1][which].astype(jnp.float32)
        for level in range(nseq - 1):
            total = total + arrived[level, last][which].astype(jnp.float32)
        totals.append(total)
    return totals


def after(x, gate):
    return lax.optimization_barrier((x, gate))[0]


def shards(tokens, gate_weight, up_weight, down_pool, up_pool, req_len, req_adapter, owner_slot):
    nseq = lax.axis_size("seq")
    ntp = lax.axis_size("tp")
    each = ntp // nseq
    me = lax.axis_index("tp")
    place = jnp.arange(ntp, dtype=jnp.int32)
    ordered = chunk_of(place // each, nseq) * each + place % each
    position = jnp.sum(jnp.where(ordered[:, None] == place[None, :], place[:, None], 0), axis=0)
    down_slot, down_here = held(
        slots_of(place, req_len, req_adapter, owner_slot), me * down_pool.shape[0], down_pool.shape[0]
    )
    up_slot, up_here = held(
        slots_of(ordered, req_len, req_adapter, owner_slot),
        lax.axis_index("seq") * up_pool.shape[0],
        up_pool.shape[0],
    )
    down_table = jnp.stack([down_slot, down_here, jnp.full_like(down_slot, me), position])
    up_table = jnp.stack([up_slot, up_here, ordered])
    columns = gate_weight.shape[1]
    tile = 256 if columns % 256 == 0 else 128
    tiles = columns // tile
    (first,), (later,) = GROUPS
    rows = first

    pieces = gather_cores(gather_chips(tokens[:rows], ntp), ntp)
    (x,), mine = assemble(pieces, (first,), down_pool, down_table, 1 << 20)
    x = x.reshape(-1, x.shape[2])
    cuts = [(w, f, c) for w in (gate_weight, up_weight) for f, c in ((0, tiles // 2), (tiles // 2, tiles - tiles // 2))]
    left = list(cuts)

    def piece(gate):
        if not left:
            return None
        weight, begin, count = left.pop(0)
        if weight is gate_weight:
            weight = pltpu.with_memory_space_constraint(weight, pltpu.HBM)
        return project(after(x, gate), weight, begin, count, tile)

    steps, parts = sum_beside(mine.reshape(-1, mine.shape[2]), "tp", ntp, piece)
    shared = steps[-1]
    chips = gather_chips(after(tokens[rows:], steps[-2]), ntp)
    sums, more = sum_beside(shared, "seq", nseq, piece)
    parts = [part for part in parts + more if part is not None]
    inner = sums[-1].reshape(mine.shape)

    def terms(parts, inner, start, rows, first, count, gate, hint=1 << 10):
        given = after(inner, gate) if gate is not None else inner
        return add_low_rank(parts, given, start, rows, first, count, up_pool, up_table, each, hint)

    def first_hop(send):
        return lax.ppermute(send, "seq", hop_pairs(0, nseq))

    head = terms(parts, inner, 0, rows, 0, 1, None)
    pieces = gather_cores(list(after(tuple(chips), head)), ntp)
    (x,), mine = assemble(pieces, (later,), down_pool, down_table, AHEAD)
    head_hop = first_hop(head)
    steps, _ = sum_beside(mine.reshape(-1, mine.shape[2]), "tp", ntp, lambda gate: None)
    shared = steps[-1]
    rest = terms(parts, inner, 0, rows, 1, nseq - 2, mine)
    kept = terms(parts, inner, 0, rows, nseq - 1, 1, rest)
    rest_hop = first_hop(after(rest, shared))
    inner = sum_one_step(shared, "seq", nseq).reshape(mine.shape)
    second = add(head[0], after(head_hop, rest)[0])
    second_hop = lax.ppermute(second, "seq", hop_pairs(1, nseq))
    x = after(x.reshape(-1, x.shape[2]), (second, kept))
    own = [head[0]] + [rest[slot] for slot in range(nseq - 2)] + [kept[0]]

    rows = later
    gate_part = project(x, gate_weight, 0, tiles, tile, AHEAD)
    parts = [gate_part, project(after(x, gate_part), up_weight, 0, tiles, tile, 1 << 10)]
    sent = [terms(parts, inner, 0, rows, 0, 1, None)]
    for slot in range(1, nseq):
        sent.append(terms(parts, inner, 0, rows, slot, 1, (sent[-1], second_hop)))
    rest_hop = after(rest_hop, sent[-1])
    third_hop = lax.ppermute(add(rest[0], rest_hop[0]), "seq", hop_pairs(1, nseq))
    hops = []
    for slot in range(nseq - 1):
        hops.append(first_hop(after(sent[slot], hops[slot - 2] if slot > 1 else rest_hop)))

    hops[0] = after(hops[0], third_hop)
    totals = [
        scatter_line(own, [head_hop[0]] + [rest_hop[slot] for slot in range(nseq - 2)], nseq, {(1, 1): second_hop, (1, 2): third_hop}),
        scatter_line([term[0] for term in sent], [hop[0] for hop in hops], nseq),
    ]
    out = [(jax.nn.silu(total[0]) * total[1]).astype(jnp.bfloat16) for total in totals]
    return jnp.concatenate(out, axis=1).reshape(-1, columns)


def solution(mesh):
    placed = (
        P("tp", "seq"),
        P("seq", "tp"),
        P("seq", "tp"),
        P("tp", None, "seq"),
        P("seq", None, None, "tp"),
        P(),
        P(),
        P(),
    )
    return jax.shard_map(
        shards, mesh=mesh, in_specs=placed, out_specs=P("seq", "tp"), check_vma=False
    )
```
